256 devices in a mesh: seq: 16 (over x, y), mp: 16 (over z, core).
Axes of the slice: x: 4, y: 4, z: 8, core: 2. Of those that a mesh axis runs over, the one named last changes fastest.
Arguments:
- features: bfloat16 [32768, 16384], P('seq', 'mp'), may hold values from -6 to 6
- coupling: bfloat16 [32768, 256], P('seq'), may hold values from -6 to 6
- gate_values: bfloat16 [32768, 16384], P('seq', 'mp'), may hold values from -40 to 40
- step_raw: float32 [256, 32768], P('mp', 'seq'), may hold values from -12 to 32768
- decay_log: float32 [256], P('mp'), may hold values from -8 to 0
- feature_taps: float32 [4, 16384], P(None, 'mp'), may hold values from -3 to 3
- feature_offset: float32 [16384], P('mp'), may hold values from -3 to 3
- coupling_taps: float32 [4, 256], replicated, may hold values from -3 to 3
- coupling_offset: float32 [256], replicated, may hold values from -3 to 3
- norm_gain: float32 [16384], P('mp'), may hold values from 0.25 to 1.75
Outputs:
- normalized: bfloat16 [32768, 16384], P('seq', 'mp')
The draws below stay inside these ranges and needn't reach their ends.
All inputs are finite; a program needn't handle non-finite values.
Results may differ from the reference program's by a relative error of at most 0.0061.
Values may be sent and summed in bfloat16 or wider, within the bound.
No kernel may reach another device: no remote copies, remote signals or barrier semaphores. Data moves between devices by JAX's collectives and lax.ppermute only.
A program may use at most 128 MiB of HBM per device.

```python
import math
import jax
import jax.numpy as jnp
from jax import lax

TOK_DEV = 2048
HEAD_TOTAL = 256
HEAD_DIM = 64
STATE = 128
KCONV = 4
BLOCK = 256
SEQUENCE_TOKENS = 32768
INNER = 16384


def decay_plan(key):
    random_key_series = jax.random.split(jax.random.fold_in(key, 101), 7)
    fast_share = 0.5
    is_fast = jax.random.uniform(random_key_series[0], (HEAD_TOTAL,)) < fast_share
    rate_fast = jnp.exp(jax.random.uniform(random_key_series[1], (HEAD_TOTAL,), minval=math.log(1.0 / 50.0), maxval=math.log(1.0 / 30.0)))
    rate_slow = jnp.exp(jax.random.uniform(random_key_series[2], (HEAD_TOTAL,), minval=math.log(0.2), maxval=math.log(0.8))) / SEQUENCE_TOKENS
    rate_value = jnp.where(is_fast, rate_fast, rate_slow)
    typical = 0.5 * jnp.sqrt(jnp.maximum(rate_value, 1.0 / SEQUENCE_TOKENS))
    spike_amplitude = rate_value / typical
    sections = SEQUENCE_TOKENS // TOK_DEV
    section_factor = jnp.exp(jax.random.uniform(random_key_series[3], (sections, HEAD_TOTAL), minval=math.log(0.5), maxval=math.log(1.5)))
    section_factor = jnp.repeat(section_factor, TOK_DEV, axis=0, total_repeat_length=SEQUENCE_TOKENS)
    jitter = jnp.exp(jax.random.uniform(random_key_series[4], (SEQUENCE_TOKENS, HEAD_TOTAL), minval=math.log(0.7), maxval=math.log(1.4)))
    increment_amount = typical[None, :] * section_factor * jitter
    spike_locations = jax.random.randint(random_key_series[5], (2,), 0, SEQUENCE_TOKENS)
    spike_penalty = jax.random.uniform(random_key_series[6], (2, HEAD_TOTAL), minval=0.2, maxval=0.35)
    spike_increment = -jnp.log1p(-spike_penalty) / spike_amplitude[None, :]
    token_locations = jnp.arange(SEQUENCE_TOKENS)
    earliest_match = (token_locations == spike_locations[0])[:, None]
    latter_match = (token_locations == spike_locations[1])[:, None]
    complete_increment = jnp.where(earliest_match, spike_increment[0][None, :], increment_amount)
    complete_increment = jnp.where(latter_match, spike_increment[1][None, :], complete_increment)
    damping = jnp.minimum(1.0, increment_amount / complete_increment)
    return (spike_amplitude, complete_increment, damping)


def draw_features(key, part):
    spike_amplitude, complete_increment, damping = decay_plan(key)
    noise_key = jax.random.fold_in(key, 202)
    noise_field = jax.random.normal(noise_key, (SEQUENCE_TOKENS, HEAD_TOTAL, HEAD_DIM))
    values = jnp.clip(noise_field * damping[:, :, None], -6.0, 6.0)
    return values.reshape(SEQUENCE_TOKENS, INNER).astype(jnp.bfloat16)


def draw_step_raw(key, part):
    spike_amplitude, complete_increment, damping = decay_plan(key)
    raw_values = complete_increment + jnp.log1p(-jnp.exp(-complete_increment))
    return raw_values.T.astype(jnp.float32)


def draw_decay_log(key, part):
    spike_amplitude, complete_increment, damping = decay_plan(key)
    return jnp.log(spike_amplitude).astype(jnp.float32)


def draw_gate_values(key, part):
    random_key_series = jax.random.split(jax.random.fold_in(key, 303), 3)
    columns = jnp.arange(INNER).astype(jnp.float32) / INNER
    row_scale = jnp.exp(jax.random.uniform(random_key_series[0], (SEQUENCE_TOKENS, 1), minval=math.log(0.5), maxval=math.log(5.0)))
    col_scale = 0.3 * jnp.power(10.0, columns)
    noise_field = jax.random.normal(random_key_series[2], (SEQUENCE_TOKENS, INNER))
    values = jnp.clip(noise_field * col_scale[None, :] * row_scale, -40.0, 40.0)
    return values.astype(jnp.bfloat16)


def block_levels(own_key, extent, shards, low, top_value):
    level = 1.0
    for axis_at, shards_of in shards:
        steps = jax.random.uniform(jax.random.fold_in(jax.random.fold_in(own_key, 6), axis_at), (shards_of,), jnp.float32, low / len(shards), top_value / len(shards))
        level = level * jnp.repeat(jnp.exp(steps), extent[axis_at] // shards_of).reshape((-1,) + (1,) * (len(extent) - 1 - axis_at))
    return level


def normal_values(own_key, shape, scale, most, cuts=(), held_as=jnp.bfloat16):
    entries = scale * jax.random.normal(own_key, shape, jnp.float32)
    if cuts:
        entries = entries * block_levels(own_key, shape, cuts, -0.22, 0.18)
    return jnp.clip(entries, -most, most).astype(held_as)


def setup_inputs(seed: int = 0) -> dict:
    streams_of = jax.random.split(jax.random.key(seed), 11)
    features = draw_features(jax.random.fold_in(streams_of[10], 71), 0)
    coupling = normal_values(streams_of[1], (SEQUENCE_TOKENS, 2 * STATE), 1.0, 6.0, ((0, 16),))
    gate_values = draw_gate_values(jax.random.fold_in(streams_of[10], 71), 0)
    step_raw = draw_step_raw(jax.random.fold_in(streams_of[10], 71), 0)
    decay_log = draw_decay_log(jax.random.fold_in(streams_of[10], 71), 0)
    feature_taps = normal_values(streams_of[5], (KCONV, INNER), KCONV ** -0.5, 3.0, ((1, 16),), jnp.float32)
    feature_offset = normal_values(streams_of[6], (INNER,), 0.5, 3.0, ((0, 16),), jnp.float32)
    coupling_taps = normal_values(streams_of[7], (KCONV, 2 * STATE), KCONV ** -0.5, 3.0, (), jnp.float32)
    coupling_offset = normal_values(streams_of[8], (2 * STATE,), 0.5, 3.0, (), jnp.float32)
    norm_gain = jnp.clip(1.0 + 0.15 * jax.random.normal(streams_of[9], (INNER,), jnp.float32), 0.25, 1.75)
    return {"features": features, "coupling": coupling, "gate_values": gate_values, "step_raw": step_raw, "decay_log": decay_log, "feature_taps": feature_taps, "feature_offset": feature_offset, "coupling_taps": coupling_taps, "coupling_offset": coupling_offset, "norm_gain": norm_gain}


FULL_PRECISION = lax.Precision.HIGHEST

def causal_mix(previous, current, weight, bias_row):
    tap_count = weight.shape[0]
    length = current.shape[0]
    padded = jnp.concatenate([previous, current], axis=0)
    running = jnp.zeros(current.shape, jnp.float32) + bias_row[None, :]
    for offset in range(tap_count):
        running = running + weight[offset][None, :] * padded[offset:offset + length].astype(jnp.float32)
    return jax.nn.silu(running).astype(jnp.bfloat16)

def block_pass(state_now, feature_block, input_map, output_map, step_block, log_block):
    head_count, block_len = step_block.shape
    feature = feature_block.shape[1] // head_count
    per_head = feature_block.astype(jnp.float32).reshape(block_len, head_count, feature)
    scores = jnp.dot(output_map, input_map.T, precision=FULL_PRECISION)
    spread = log_block[:, :, None] - log_block[:, None, :]
    causal = (jnp.arange(block_len)[:, None] >= jnp.arange(block_len)[None, :])[None, :, :]
    weights = jnp.where(causal, jnp.exp(jnp.where(causal, spread, 0.0)), 0.0)
    weights = weights * scores[None, :, :] * step_block[:, None, :]
    inside = jnp.einsum('hts,shp->thp', weights, per_head, precision=FULL_PRECISION)
    carried = jnp.einsum('tn,hpn->thp', output_map, state_now, precision=FULL_PRECISION)
    carried = carried * jnp.exp(log_block).T[:, :, None]
    ending = log_block[:, -1]
    to_end = jnp.exp(ending[:, None] - log_block) * step_block
    weighted = per_head * to_end.T[:, :, None]
    fresh_part = jnp.einsum('shp,sn->hpn', weighted, input_map, precision=FULL_PRECISION)
    new_state = jnp.exp(ending)[:, None, None] * state_now + fresh_part
    return (new_state, (inside + carried).reshape(block_len, head_count * feature))

def reference(features, coupling, gate_values, step_raw, decay_log, feature_taps, feature_offset, coupling_taps, coupling_offset, norm_gain):
    tap_count = feature_taps.shape[0]
    head_count = decay_log.shape[0]
    state_size = coupling.shape[1] // 2
    feature = features.shape[1] // head_count
    blocks = SEQUENCE_TOKENS // BLOCK
    rate_values = jnp.exp(decay_log)

    def advance(carried_in, inputs):
        state_now, prior_features, prior_coupling = carried_in
        feature_block, coupling_block, gate_block, raw_block = inputs
        filtered = causal_mix(prior_features, feature_block, feature_taps, feature_offset)
        coupled = causal_mix(prior_coupling, coupling_block, coupling_taps, coupling_offset).astype(jnp.float32)
        step_block = jax.nn.softplus(raw_block)
        log_block = jnp.cumsum(-rate_values[:, None] * step_block, axis=1)
        new_state, output = block_pass(state_now, filtered, coupled[:, :state_size], coupled[:, state_size:], step_block, log_block)
        gated_values = output * jax.nn.silu(gate_block.astype(jnp.float32))
        mean_square = lax.optimization_barrier(jnp.mean(gated_values * gated_values, axis=1))
        result = (gated_values * norm_gain[None, :] * lax.rsqrt(mean_square + 1e-05)[:, None]).astype(jnp.bfloat16)
        tail_rows = tap_count - 1
        return ((new_state, feature_block[BLOCK - tail_rows:], coupling_block[BLOCK - tail_rows:]), result)
    zero_state = jnp.zeros((head_count, feature, state_size), jnp.float32)
    prior_features = jnp.zeros((tap_count - 1, features.shape[1]), jnp.bfloat16)
    prior_coupling = jnp.zeros((tap_count - 1, coupling.shape[1]), jnp.bfloat16)
    inputs = (features.reshape(blocks, BLOCK, features.shape[1]), coupling.reshape(blocks, BLOCK, coupling.shape[1]), gate_values.reshape(blocks, BLOCK, gate_values.shape[1]), step_raw.reshape(head_count, blocks, BLOCK).transpose(1, 0, 2))
    final_carry, results = lax.scan(advance, (zero_state, prior_features, prior_coupling), inputs)
    return results.reshape(SEQUENCE_TOKENS, features.shape[1])
```

```python
import functools
import math

import jax
import jax.numpy as jnp
import numpy as np
from jax import lax
from jax.experimental import pallas as pl
from jax.experimental.pallas import tpu as pltpu
from jax.sharding import PartitionSpec as P

CHUNK = 128
LANES = 128
HALO = 8
HEAD_DIM = 64
LOG2E = math.log2(math.e)
BF16 = jnp.bfloat16
F32 = jnp.float32


def params(mib):
    return pltpu.CompilerParams(vmem_limit_bytes=mib << 20)


def cost(flops, nbytes, trans=0):
    return pl.CostEstimate(flops=flops, bytes_accessed=nbytes, transcendentals=trans)


def silu(v):
    half = 0.5 * v
    return half + half * jnp.tanh(half)


def split(v):
    high = v.astype(BF16)
    return high, (v - high.astype(F32)).astype(BF16)


def contract_rows(a, b):
    return lax.dot_general(a, b, (((0,), (0,)), ((), ())), preferred_element_type=F32)


def contract_lanes(a, b):
    return lax.dot_general(a, b, (((1,), (1,)), ((), ())), preferred_element_type=F32)


def decay_kernel(raw_ref, mag_ref, tri_ref, row_ref, wtot_ref, ex_ref, dsec_ref):
    heads, tokens = raw_ref.shape
    chunks = tokens // CHUNK
    raw = raw_ref[...]
    small = jnp.exp(-jnp.abs(raw))
    grown = 1.0 + small
    rest = grown - 1.0
    safe = jnp.where(rest == 0.0, 1.0, rest)
    log1p = jnp.where(rest == 0.0, small, jnp.log(grown) * (small / safe))
    step = jnp.maximum(raw, 0.0) + log1p
    slope = -jnp.exp(mag_ref[...]) * LOG2E
    stacked = jnp.concatenate(
        [step[:, c * CHUNK : (c + 1) * CHUNK] for c in range(chunks)], axis=0
    )
    slopes = jnp.concatenate([slope] * chunks, axis=0)
    sums = jnp.dot(
        stacked * slopes, tri_ref[...], precision=lax.Precision.HIGHEST, preferred_element_type=F32
    )
    before = jnp.zeros((heads, 1), F32)
    befores, totals = [], []
    for c in range(chunks):
        befores.append(before)
        total = sums[c * heads : (c + 1) * heads, CHUNK - 1 : CHUNK]
        totals.append(total)
        before = before + total
    afters = [None] * chunks
    after = jnp.zeros((heads, 1), F32)
    for c in reversed(range(chunks)):
        afters[c] = after
        after = after + totals[c]
    for c in range(chunks):
        rows = slice(c * heads, (c + 1) * heads)
        upto = sums[rows, :CHUNK]
        beyond = sums[rows, CHUNK:]
        amount = stacked[rows]
        row_ref[c, 0:heads] = upto
        row_ref[c, heads : 2 * heads] = amount
        high, low = split(amount * jnp.exp2(beyond + afters[c]))
        wtot_ref[c, 0:heads] = high
        wtot_ref[c, heads : 2 * heads] = low
        for k, v in enumerate(
            (amount * jnp.exp2(beyond), jnp.exp2(upto), jnp.exp2(upto + befores[c]))
        ):
            high, low = split(v)
            ex_ref[c, (2 * k) * heads : (2 * k + 1) * heads] = high
            ex_ref[c, (2 * k + 1) * heads : (2 * k + 2) * heads] = low
    whole = jnp.broadcast_to(jnp.exp2(before), (heads, LANES))
    high, low = split(whole)
    lane = lax.broadcasted_iota(jnp.int32, (heads, LANES), 1)
    dsec_ref[0:heads] = jnp.where(lane == 0, high.astype(F32), 0.0).astype(BF16)
    dsec_ref[heads : 2 * heads] = jnp.where(lane == 1, low.astype(F32), 0.0).astype(BF16)


def mixed(ext_ref, tile, length, taps, bias):
    start = HALO - 3
    running = jnp.broadcast_to(bias, (length, LANES))
    for k in range(4):
        running = running + taps[k : k + 1] * ext_ref[tile, start + k : start + k + length, :]
    return silu(running)


def ends_kernel(
    feat_ref, coup_ref, halo_ref, taps_ref, bias_ref, ctaps_ref, cbias_ref, wtot_ref, dsec_ref, spread_ref,
    filt_ref, coupled_ref, pay_ref, ext_ref, weighted_ref, acc_ref,
):
    i = pl.program_id(0)
    length, channels = feat_ref.shape
    tiles = channels // LANES
    ctiles = coup_ref.shape[1] // LANES

    @pl.when(i == 0)
    def _():
        for j in range(tiles + ctiles):
            ext_ref[j, 0:HALO, :] = halo_ref[:, j * LANES : (j + 1) * LANES].astype(F32)
        acc_ref[...] = jnp.zeros_like(acc_ref)

    @pl.when(i > 0)
    def _():
        for j in range(tiles + ctiles):
            ext_ref[j, 0:HALO, :] = ext_ref[j, length : length + HALO, :]

    for j in range(ctiles):
        lanes = slice(j * LANES, (j + 1) * LANES)
        ext_ref[tiles + j, HALO : HALO + length, :] = coup_ref[:, lanes].astype(F32)
        coupled_ref[:, lanes] = mixed(
            ext_ref, tiles + j, length, ctaps_ref[:, lanes], cbias_ref[:, lanes]
        ).astype(BF16)
    for j in range(tiles):
        lanes = slice(j * LANES, (j + 1) * LANES)
        ext_ref[j, HALO : HALO + length, :] = feat_ref[:, lanes].astype(F32)
        value = mixed(ext_ref, j, length, taps_ref[:, lanes], bias_ref[:, lanes]).astype(BF16)
        filt_ref[:, lanes] = value
    for c in range(length // CHUNK):
        rows = slice(c * CHUNK, (c + 1) * CHUNK)
        scale = contract_rows(wtot_ref[c], spread_ref[...])
        weighted_ref[rows] = (filt_ref[rows].astype(F32) * scale).astype(BF16)
    acc_ref[...] += contract_rows(coupled_ref[:, :LANES], weighted_ref[...])

    @pl.when(i == pl.num_programs(0) - 1)
    def _():
        decays = contract_rows(dsec_ref[...], spread_ref[...])[0:8].astype(BF16)
        parts = pay_ref.shape[0]
        share = LANES // parts
        for j in range(parts):
            pay_ref[j, 0:share] = acc_ref[j * share : (j + 1) * share].astype(BF16)
            pay_ref[j, share : share + 8] = decays


def relay_kernel(pay_ref, order_ref, out_ref):
    parts, rows, _ = pay_ref.shape
    share = rows - 8
    entering = jnp.zeros(out_ref.shape[1:], F32)
    for j in range(parts):
        out_ref[j] = entering.astype(BF16)
        tail = pay_ref[j, share : share + 8].astype(F32)
        decay = tail[0:1] + tail[1:2]
        entering = decay * entering + pay_ref[j, 0:share].astype(F32)


def inside_kernel(
    filt_ref, coupled_ref, gate_ref, row_ref, ex_ref, spread_ref, state_ref, order_ref, *rest
):
    yg_ref, gp_ref, end_ref, narrow_ref = rest[-4:]
    i = pl.program_id(0)
    heads = row_ref.shape[1] // 2
    channels = filt_ref.shape[1]

    @pl.when(i == 0)
    def _():
        end_ref[...] = state_ref[...]

    inputs = coupled_ref[:, :LANES]
    reads = coupled_ref[:, LANES:]
    above = lax.broadcasted_iota(jnp.int32, (CHUNK, CHUNK), 0)
    below = lax.broadcasted_iota(jnp.int32, (CHUNK, CHUNK), 1)
    scores = jnp.where(above >= below, contract_lanes(reads, inputs), 0.0)
    rows = row_ref[0, 0:heads]
    amounts = row_ref[0, heads : 2 * heads]
    columns = rows.T
    lane = lax.broadcasted_iota(jnp.int32, (1, LANES), 1)
    left = jnp.where(lane < HEAD_DIM, 1.0, 0.0)
    right = 1.0 - left
    narrow_ref[...] = end_ref[...].astype(BF16)
    width = 2 * LANES
    for q in range(channels // width):
        lanes = slice(q * width, (q + 1) * width)
        spread = spread_ref[:, lanes]
        x = filt_ref[:, lanes].astype(F32)
        decayed = contract_rows(ex_ref[0, 2 * heads : 4 * heads], spread)
        carried = jnp.dot(reads, narrow_ref[:, lanes], preferred_element_type=F32) * decayed
        last = decayed[CHUNK - 1 : CHUNK]
        weighted = (x * contract_rows(ex_ref[0, 0 : 2 * heads], spread)).astype(BF16)
        end_ref[:, lanes] = end_ref[:, lanes] * last + contract_rows(inputs, weighted)
        parts = []
        for p in range(2):
            weights = []
            for h in (4 * q + 2 * p, 4 * q + 2 * p + 1):
                gap = jnp.minimum(columns[:, h : h + 1] - rows[h : h + 1], 0.0)
                weights.append((jnp.exp2(gap) * scores * amounts[h : h + 1]).astype(BF16))
            pair = x[:, p * LANES : (p + 1) * LANES]
            block = jnp.concatenate([(pair * left).astype(BF16), (pair * right).astype(BF16)], axis=0)
            parts.append(
                jnp.dot(jnp.concatenate(weights, axis=1), block, preferred_element_type=F32)
            )
        total = carried + jnp.concatenate(parts, axis=1)
        opened = silu(gate_ref[:, lanes].astype(F32))
        yg_ref[:, lanes] = (total * opened).astype(BF16)
        running = contract_rows(ex_ref[0, 4 * heads : 6 * heads], spread)
        gp_ref[:, lanes] = (opened * running).astype(BF16)


def gated_kernel(read_ref, enter_ref, yg_ref, gp_ref, gated_ref, out_ref, sums_ref):
    i = pl.program_id(0)
    length, channels = yg_ref.shape
    before = jnp.dot(read_ref[...], enter_ref[...], preferred_element_type=F32)
    gated = yg_ref[...].astype(F32) + gp_ref[...].astype(F32) * before
    gated_ref[...] = gated.astype(BF16)
    ones = jnp.ones((8, channels), BF16)
    squares = contract_lanes(ones, (gated * gated).astype(BF16))
    for c in range(length // CHUNK):
        sums_ref[pl.ds(i * (length // CHUNK) + c, 1), :] = squares[0:1, c * CHUNK : (c + 1) * CHUNK]

    @pl.when(i == pl.num_programs(0) - 1)
    def _():
        mine = sums_ref[...].astype(out_ref.dtype)
        for j in range(out_ref.shape[0]):
            out_ref[j] = mine


def normal_kernel(inner, gated_ref, sums_ref, gain_ref, out_ref, scale_ref):
    i = pl.program_id(0)
    length, channels = gated_ref.shape
    chunks = sums_ref.shape[1]

    @pl.when(i == 0)
    def _():
        total = sums_ref[0].astype(F32)
        for j in range(1, sums_ref.shape[0]):
            total = total + sums_ref[j].astype(F32)
        columns = lax.rsqrt(total / inner + 1e-05).T
        for c in range(chunks):
            scale_ref[c] = jnp.broadcast_to(columns[:, c : c + 1], (CHUNK, LANES))

    per = length // CHUNK
    for c in range(per):
        rows = slice(c * CHUNK, (c + 1) * CHUNK)
        scale = scale_ref[i * per + c]
        for j in range(channels // LANES):
            lanes = slice(j * LANES, (j + 1) * LANES)
            out_ref[rows, lanes] = (
                gated_ref[rows, lanes].astype(F32) * gain_ref[:, lanes] * scale
            ).astype(BF16)


def whole(shape):
    return pl.BlockSpec(shape, lambda i: (0,) * len(shape))


def on_device(
    features,
    coupling,
    gate_values,
    step_raw,
    decay_log,
    feature_taps,
    feature_offset,
    coupling_taps,
    coupling_offset,
    norm_gain,
):
    tokens, channels = features.shape
    heads = decay_log.shape[0]
    sections = lax.axis_size("seq")
    groups = lax.axis_size("mp")
    chunks = tokens // CHUNK
    share = LANES // sections
    any_spec = pl.BlockSpec(memory_space=pl.ANY)

    tail = jnp.concatenate([features[tokens - HALO :], coupling[tokens - HALO :]], axis=1)
    halo = lax.ppermute(tail, "seq", [(i, i + 1) for i in range(sections - 1)])

    order = np.arange(CHUNK)
    tri = np.concatenate(
        [order[:, None] <= order[None, :], order[:, None] > order[None, :]], axis=1
    ).astype(np.float32)
    one = np.arange(channels)[None, :] // HEAD_DIM == np.arange(heads)[:, None]
    spread = jnp.asarray(np.concatenate([one, one], axis=0), BF16)

    rows, wtot, ex, dsec = pl.pallas_call(
        decay_kernel,
        out_shape=(
            jax.ShapeDtypeStruct((chunks, 2 * heads, CHUNK), F32),
            jax.ShapeDtypeStruct((chunks, 2 * heads, CHUNK), BF16),
            jax.ShapeDtypeStruct((chunks, 6 * heads, CHUNK), BF16),
            jax.ShapeDtypeStruct((2 * heads, LANES), BF16),
        ),
        compiler_params=params(8),
        cost_estimate=cost(10**7, 10**6, 10**5),
    )(step_raw, decay_log[:, None], jnp.asarray(tri))

    block = 2 * CHUNK
    filtered, coupled, ends = pl.pallas_call(
        ends_kernel,
        grid=(tokens // block,),
        in_specs=[
            pl.BlockSpec((block, channels), lambda i: (i, 0)),
            pl.BlockSpec((block, 2 * LANES), lambda i: (i, 0)),
            whole((HALO, channels + 2 * LANES)),
            whole((4, channels)),
            whole((1, channels)),
            whole((4, 2 * LANES)),
            whole((1, 2 * LANES)),
            pl.BlockSpec((2, 2 * heads, CHUNK), lambda i: (i, 0, 0)),
            whole((2 * heads, LANES)),
            whole((2 * heads, channels)),
        ],
        out_specs=(
            pl.BlockSpec((block, channels), lambda i: (i, 0)),
            pl.BlockSpec((block, 2 * LANES), lambda i: (i, 0)),
            whole((sections, share + 8, channels)),
        ),
        out_shape=(
            jax.ShapeDtypeStruct((tokens, channels), BF16),
            jax.ShapeDtypeStruct((tokens, 2 * LANES), BF16),
            jax.ShapeDtypeStruct((sections, share + 8, channels), BF16),
        ),
        scratch_shapes=[
            pltpu.VMEM((channels // LANES + 2, HALO + block, LANES), F32),
            pltpu.VMEM((block, channels), BF16),
            pltpu.VMEM((LANES, channels), F32),
        ],
        compiler_params=params(24),
        cost_estimate=cost(10**9, 10**7, 2 * 10**6),
    )(
        features,
        coupling,
        halo,
        feature_taps,
        feature_offset[None, :],
        coupling_taps,
        coupling_offset[None, :],
        wtot,
        dsec,
        spread,
    )

    def inside(first, count, state, order, *held):
        return pl.pallas_call(
            inside_kernel,
            grid=(count,),
            in_specs=[
                pl.BlockSpec((CHUNK, channels), lambda i: (first + i, 0)),
                pl.BlockSpec((CHUNK, 2 * LANES), lambda i: (first + i, 0)),
                pl.BlockSpec((CHUNK, channels), lambda i: (first + i, 0)),
                pl.BlockSpec((1, 2 * heads, CHUNK), lambda i: (first + i, 0, 0)),
                pl.BlockSpec((1, 6 * heads, CHUNK), lambda i: (first + i, 0, 0)),
                whole((2 * heads, channels)),
                whole((LANES, channels)),
                any_spec,
            ]
            + [any_spec] * len(held),
            out_specs=(
                pl.BlockSpec((CHUNK, channels), lambda i: (first + i, 0)),
                pl.BlockSpec((CHUNK, channels), lambda i: (first + i, 0)),
                whole((LANES, channels)),
            ),
            out_shape=(
                jax.ShapeDtypeStruct((tokens, channels), BF16),
                jax.ShapeDtypeStruct((tokens, channels), BF16),
                jax.ShapeDtypeStruct((LANES, channels), F32),
            ),
            input_output_aliases={8 + k: k for k in range(len(held))},
            scratch_shapes=[pltpu.VMEM((LANES, channels), BF16)],
            compiler_params=params(24),
            cost_estimate=cost(count * 3 * 10**8, count * 10**6, count * 4 * 10**5),
        )(filtered, coupled, gate_values, rows, ex, spread, state, order, *held)

    half = chunks // 2
    gathered = lax.all_to_all(ends, "seq", 0, 0, tiled=True)
    yg, gp, state = inside(0, half, jnp.zeros((LANES, channels), F32), dsec)
    starts = pl.pallas_call(
        relay_kernel,
        grid=(1,),
        in_specs=[whole((sections, share + 8, channels)), any_spec],
        out_specs=whole((sections, share, channels)),
        out_shape=jax.ShapeDtypeStruct((sections, share, channels), BF16),
        compiler_params=params(8),
        cost_estimate=cost(10**6, 10**6),
    )(gathered, state)
    entering = lax.all_to_all(starts, "seq", 0, 0, tiled=True).reshape(LANES, channels)
    yg, gp, _ = inside(half, chunks - half, state, starts, yg, gp)

    gated, squares = pl.pallas_call(
        gated_kernel,
        grid=(tokens // block,),
        in_specs=[
            pl.BlockSpec((block, LANES), lambda i: (i, 1)),
            whole((LANES, channels)),
            pl.BlockSpec((block, channels), lambda i: (i, 0)),
            pl.BlockSpec((block, channels), lambda i: (i, 0)),
        ],
        out_specs=(
            pl.BlockSpec((block, channels), lambda i: (i, 0)),
            whole((groups, chunks, CHUNK)),
        ),
        out_shape=(
            jax.ShapeDtypeStruct((tokens, channels), BF16),
            jax.ShapeDtypeStruct((groups, chunks, CHUNK), F32),
        ),
        scratch_shapes=[pltpu.VMEM((chunks, CHUNK), F32)],
        compiler_params=params(16),
        cost_estimate=cost(6 * 10**8, 12 * 10**6),
    )(coupled, entering, yg, gp)
    squares = lax.all_to_all(squares, "mp", 0, 0, tiled=True)

    return pl.pallas_call(
        functools.partial(normal_kernel, float(channels * groups)),
        grid=(tokens // block,),
        in_specs=[
            pl.BlockSpec((block, channels), lambda i: (i, 0)),
            whole((groups, chunks, CHUNK)),
            whole((1, channels)),
        ],
        out_specs=pl.BlockSpec((block, channels), lambda i: (i, 0)),
        out_shape=jax.ShapeDtypeStruct((tokens, channels), BF16),
        scratch_shapes=[pltpu.VMEM((chunks, CHUNK, LANES), F32)],
        compiler_params=params(16),
        cost_estimate=cost(10**7, 8 * 10**6),
    )(gated, squares, norm_gain[None, :])


def solution(mesh):
    in_specs = (
        P("seq", "mp"),
        P("seq", None),
        P("seq", "mp"),
        P("mp", "seq"),
        P("mp"),
        P(None, "mp"),
        P("mp"),
        P(),
        P(),
        P("mp"),
    )
    out_specs = P("seq", "mp")
    return jax.shard_map(
        on_device, mesh=mesh, in_specs=in_specs, out_specs=out_specs, check_vma=False
    )
```

```python
import functools
import math

import jax
import jax.numpy as jnp
import numpy as np
from jax import lax
from jax.experimental import pallas as pl
from jax.experimental.pallas import tpu as pltpu
from jax.sharding import PartitionSpec as P

CHUNK = 128
LANES = 128
HALO = 8
HEAD_DIM = 64
LOG2E = math.log2(math.e)
BF16 = jnp.bfloat16
F32 = jnp.float32


def params(mib):
    return pltpu.CompilerParams(vmem_limit_bytes=60 << 20)


def cost(flops, nbytes, trans=0):
    return pl.CostEstimate(flops=flops, bytes_accessed=nbytes, transcendentals=trans)


def silu(v):
    half = 0.5 * v
    return half + half * jnp.tanh(half)


def split(v):
    high = v.astype(BF16)
    return high, (v - high.astype(F32)).astype(BF16)


def contract_rows(a, b):
    return lax.dot_general(a, b, (((0,), (0,)), ((), ())), preferred_element_type=F32)


def contract_lanes(a, b):
    return lax.dot_general(a, b, (((1,), (1,)), ((), ())), preferred_element_type=F32)


def decay_kernel(raw_ref, mag_ref, tri_ref, row_ref, wtot_ref, ex_ref, dsec_ref):
    heads, tokens = raw_ref.shape
    chunks = tokens // CHUNK
    raw = raw_ref[...]
    small = jnp.exp(-jnp.abs(raw))
    grown = 1.0 + small
    rest = grown - 1.0
    safe = jnp.where(rest == 0.0, 1.0, rest)
    log1p = jnp.where(rest == 0.0, small, jnp.log(grown) * (small / safe))
    step = jnp.maximum(raw, 0.0) + log1p
    slope = -jnp.exp(mag_ref[...]) * LOG2E
    stacked = jnp.concatenate(
        [step[:, c * CHUNK : (c + 1) * CHUNK] for c in range(chunks)], axis=0
    )
    slopes = jnp.concatenate([slope] * chunks, axis=0)
    sums = jnp.dot(
        stacked * slopes, tri_ref[...], precision=lax.Precision.HIGHEST, preferred_element_type=F32
    )
    before = jnp.zeros((heads, 1), F32)
    befores, totals = [], []
    for c in range(chunks):
        befores.append(before)
        total = sums[c * heads : (c + 1) * heads, CHUNK - 1 : CHUNK]
        totals.append(total)
        before = before + total
    afters = [None] * chunks
    after = jnp.zeros((heads, 1), F32)
    for c in reversed(range(chunks)):
        afters[c] = after
        after = after + totals[c]
    for c in range(chunks):
        rows = slice(c * heads, (c + 1) * heads)
        upto = sums[rows, :CHUNK]
        beyond = sums[rows, CHUNK:]
        amount = stacked[rows]
        row_ref[c, 0:heads] = upto
        row_ref[c, heads : 2 * heads] = amount
        high, low = split(amount * jnp.exp2(beyond + afters[c]))
        wtot_ref[c, 0:heads] = high
        wtot_ref[c, heads : 2 * heads] = low
        for k, v in enumerate(
            (amount * jnp.exp2(beyond), jnp.exp2(upto), jnp.exp2(upto + befores[c]))
        ):
            high, low = split(v)
            ex_ref[c, (2 * k) * heads : (2 * k + 1) * heads] = high
            ex_ref[c, (2 * k + 1) * heads : (2 * k + 2) * heads] = low
    whole = jnp.broadcast_to(jnp.exp2(before), (heads, LANES))
    high, low = split(whole)
    lane = lax.broadcasted_iota(jnp.int32, (heads, LANES), 1)
    dsec_ref[0:heads] = jnp.where(lane == 0, high.astype(F32), 0.0).astype(BF16)
    dsec_ref[heads : 2 * heads] = jnp.where(lane == 1, low.astype(F32), 0.0).astype(BF16)


def mixed(ext_ref, tile, length, taps, bias):
    start = HALO - 3
    running = jnp.broadcast_to(bias, (length, LANES))
    for k in range(4):
        running = running + taps[k : k + 1] * ext_ref[tile, start + k : start + k + length, :]
    return silu(running)


def ends_kernel(
    feat_ref, coup_ref, halo_ref, taps_ref, bias_ref, ctaps_ref, cbias_ref, wtot_ref, dsec_ref, spread_ref,
    filt_ref, coupled_ref, pay_ref, ext_ref, weighted_ref, acc_ref,
):
    i = pl.program_id(0)
    length, channels = feat_ref.shape
    tiles = channels // LANES
    ctiles = coup_ref.shape[1] // LANES

    @pl.when(i == 0)
    def _():
        for j in range(tiles + ctiles):
            ext_ref[j, 0:HALO, :] = halo_ref[:, j * LANES : (j + 1) * LANES].astype(F32)
        acc_ref[...] = jnp.zeros_like(acc_ref)

    @pl.when(i > 0)
    def _():
        for j in range(tiles + ctiles):
            ext_ref[j, 0:HALO, :] = ext_ref[j, length : length + HALO, :]

    for j in range(ctiles):
        lanes = slice(j * LANES, (j + 1) * LANES)
        ext_ref[tiles + j, HALO : HALO + length, :] = coup_ref[:, lanes].astype(F32)
        coupled_ref[:, lanes] = mixed(
            ext_ref, tiles + j, length, ctaps_ref[:, lanes], cbias_ref[:, lanes]
        ).astype(BF16)
    for j in range(tiles):
        lanes = slice(j * LANES, (j + 1) * LANES)
        ext_ref[j, HALO : HALO + length, :] = feat_ref[:, lanes].astype(F32)
        value = mixed(ext_ref, j, length, taps_ref[:, lanes], bias_ref[:, lanes]).astype(BF16)
        filt_ref[:, lanes] = value
    for c in range(length // CHUNK):
        rows = slice(c * CHUNK, (c + 1) * CHUNK)
        scale = contract_rows(wtot_ref[c], spread_ref[...])
        weighted_ref[rows] = (filt_ref[rows].astype(F32) * scale).astype(BF16)
    acc_ref[...] += contract_rows(coupled_ref[:, :LANES], weighted_ref[...])

    @pl.when(i == pl.num_programs(0) - 1)
    def _():
        decays = contract_rows(dsec_ref[...], spread_ref[...])[0:8].astype(BF16)
        parts = pay_ref.shape[0]
        share = LANES // parts
        for j in range(parts):
            pay_ref[j, 0:share] = acc_ref[j * share : (j + 1) * share].astype(BF16)
            pay_ref[j, share : share + 8] = decays


def relay_kernel(pay_ref, order_ref, out_ref):
    parts, rows, _ = pay_ref.shape
    share = rows - 8
    entering = jnp.zeros(out_ref.shape[1:], F32)
    for j in range(parts):
        out_ref[j] = entering.astype(BF16)
        tail = pay_ref[j, share : share + 8].astype(F32)
        decay = tail[0:1] + tail[1:2]
        entering = decay * entering + pay_ref[j, 0:share].astype(F32)


def inside_kernel(
    filt_ref, coupled_ref, gate_ref, row_ref, ex_ref, spread_ref, state_ref, order_ref, *rest
):
    yg_ref, gp_ref, end_ref, narrow_ref = rest[-4:]
    i = pl.program_id(0)
    heads = row_ref.shape[1] // 2
    channels = filt_ref.shape[1]

    @pl.when(i == 0)
    def _():
        end_ref[...] = state_ref[...]

    inputs = coupled_ref[:, :LANES]
    reads = coupled_ref[:, LANES:]
    above = lax.broadcasted_iota(jnp.int32, (CHUNK, CHUNK), 0)
    below = lax.broadcasted_iota(jnp.int32, (CHUNK, CHUNK), 1)
    scores = jnp.where(above >= below, contract_lanes(reads, inputs), 0.0)
    rows = row_ref[0, 0:heads]
    amounts = row_ref[0, heads : 2 * heads]
    columns = rows.T
    lane = lax.broadcasted_iota(jnp.int32, (1, LANES), 1)
    left = jnp.where(lane < HEAD_DIM, 1.0, 0.0)
    right = 1.0 - left
    narrow_ref[...] = end_ref[...].astype(BF16)
    width = 2 * LANES
    for q in range(channels // width):
        lanes = slice(q * width, (q + 1) * width)
        spread = spread_ref[:, lanes]
        x = filt_ref[:, lanes].astype(F32)
        decayed = contract_rows(ex_ref[0, 2 * heads : 4 * heads], spread)
        carried = jnp.dot(reads, narrow_ref[:, lanes], preferred_element_type=F32) * decayed
        last = decayed[CHUNK - 1 : CHUNK]
        weighted = (x * contract_rows(ex_ref[0, 0 : 2 * heads], spread)).astype(BF16)
        end_ref[:, lanes] = end_ref[:, lanes] * last + contract_rows(inputs, weighted)
        parts = []
        for p in range(2):
            weights = []
            for h in (4 * q + 2 * p, 4 * q + 2 * p + 1):
                gap = jnp.minimum(columns[:, h : h + 1] - rows[h : h + 1], 0.0)
                weights.append((jnp.exp2(gap) * scores * amounts[h : h + 1]).astype(BF16))
            pair = x[:, p * LANES : (p + 1) * LANES]
            block = jnp.concatenate([(pair * left).astype(BF16), (pair * right).astype(BF16)], axis=0)
            parts.append(
                jnp.dot(jnp.concatenate(weights, axis=1), block, preferred_element_type=F32)
            )
        total = carried + jnp.concatenate(parts, axis=1)
        opened = silu(gate_ref[:, lanes].astype(F32))
        yg_ref[:, lanes] = (total * opened).astype(BF16)
        running = contract_rows(ex_ref[0, 4 * heads : 6 * heads], spread)
        gp_ref[:, lanes] = (opened * running).astype(BF16)


def gated_kernel(read_ref, enter_ref, yg_ref, gp_ref, gated_ref, out_ref, sums_ref):
    i = pl.program_id(0)
    length, channels = yg_ref.shape
    before = jnp.dot(read_ref[...], enter_ref[...], preferred_element_type=F32)
    gated = yg_ref[...].astype(F32) + gp_ref[...].astype(F32) * before
    gated_ref[...] = gated.astype(BF16)
    ones = jnp.ones((8, channels), BF16)
    squares = contract_lanes(ones, (gated * gated).astype(BF16))
    for c in range(length // CHUNK):
        sums_ref[pl.ds(i * (length // CHUNK) + c, 1), :] = squares[0:1, c * CHUNK : (c + 1) * CHUNK]

    @pl.when(i == pl.num_programs(0) - 1)
    def _():
        mine = sums_ref[...].astype(out_ref.dtype)
        for j in range(out_ref.shape[0]):
            out_ref[j] = mine


def normal_kernel(inner, gated_ref, sums_ref, gain_ref, out_ref, scale_ref):
    i = pl.program_id(0)
    length, channels = gated_ref.shape
    chunks = sums_ref.shape[1]

    @pl.when(i == 0)
    def _():
        total = sums_ref[0].astype(F32)
        for j in range(1, sums_ref.shape[0]):
            total = total + sums_ref[j].astype(F32)
        columns = lax.rsqrt(total / inner + 1e-05).T
        for c in range(chunks):
            scale_ref[c] = jnp.broadcast_to(columns[:, c : c + 1], (CHUNK, LANES))

    per = length // CHUNK
    for c in range(per):
        rows = slice(c * CHUNK, (c + 1) * CHUNK)
        scale = scale_ref[i * per + c]
        for j in range(channels // LANES):
            lanes = slice(j * LANES, (j + 1) * LANES)
            out_ref[rows, lanes] = (
                gated_ref[rows, lanes].astype(F32) * gain_ref[:, lanes] * scale
            ).astype(BF16)


def whole(shape):
    return pl.BlockSpec(shape, lambda i: (0,) * len(shape))


def on_device(
    features,
    coupling,
    gate_values,
    step_raw,
    decay_log,
    feature_taps,
    feature_offset,
    coupling_taps,
    coupling_offset,
    norm_gain,
):
    tokens, channels = features.shape
    heads = decay_log.shape[0]
    sections = lax.axis_size("seq")
    groups = lax.axis_size("mp")
    chunks = tokens // CHUNK
    share = LANES // sections
    any_spec = pl.BlockSpec(memory_space=pl.ANY)

    tail = jnp.concatenate([features[tokens - HALO :], coupling[tokens - HALO :]], axis=1)
    halo = lax.ppermute(tail, "seq", [(i, i + 1) for i in range(sections - 1)])

    order = np.arange(CHUNK)
    tri = np.concatenate(
        [order[:, None] <= order[None, :], order[:, None] > order[None, :]], axis=1
    ).astype(np.float32)
    one = np.arange(channels)[None, :] // HEAD_DIM == np.arange(heads)[:, None]
    spread = jnp.asarray(np.concatenate([one, one], axis=0), BF16)

    rows, wtot, ex, dsec = pl.pallas_call(
        decay_kernel,
        out_shape=(
            jax.ShapeDtypeStruct((chunks, 2 * heads, CHUNK), F32),
            jax.ShapeDtypeStruct((chunks, 2 * heads, CHUNK), BF16),
            jax.ShapeDtypeStruct((chunks, 6 * heads, CHUNK), BF16),
            jax.ShapeDtypeStruct((2 * heads, LANES), BF16),
        ),
        compiler_params=params(8),
        cost_estimate=cost(10**7, 10**6, 10**5),
    )(step_raw, decay_log[:, None], jnp.asarray(tri))

    block = 2 * CHUNK
    filtered, coupled, ends = pl.pallas_call(
        ends_kernel,
        grid=(tokens // block,),
        in_specs=[
            pl.BlockSpec((block, channels), lambda i: (i, 0)),
            pl.BlockSpec((block, 2 * LANES), lambda i: (i, 0)),
            whole((HALO, channels + 2 * LANES)),
            whole((4, channels)),
            whole((1, channels)),
            whole((4, 2 * LANES)),
            whole((1, 2 * LANES)),
            pl.BlockSpec((2, 2 * heads, CHUNK), lambda i: (i, 0, 0)),
            whole((2 * heads, LANES)),
            whole((2 * heads, channels)),
        ],
        out_specs=(
            pl.BlockSpec((block, channels), lambda i: (i, 0)),
            pl.BlockSpec((block, 2 * LANES), lambda i: (i, 0)),
            whole((sections, share + 8, channels)),
        ),
        out_shape=(
            jax.ShapeDtypeStruct((tokens, channels), BF16),
            jax.ShapeDtypeStruct((tokens, 2 * LANES), BF16),
            jax.ShapeDtypeStruct((sections, share + 8, channels), BF16),
        ),
        scratch_shapes=[
            pltpu.VMEM((channels // LANES + 2, HALO + block, LANES), F32),
            pltpu.VMEM((block, channels), BF16),
            pltpu.VMEM((LANES, channels), F32),
        ],
        compiler_params=params(24),
        cost_estimate=cost(10**9, 10**7, 2 * 10**6),
    )(
        features,
        coupling,
        halo,
        feature_taps,
        feature_offset[None, :],
        coupling_taps,
        coupling_offset[None, :],
        wtot,
        dsec,
        spread,
    )

    def inside(first, count, state, order, *held):
        return pl.pallas_call(
            inside_kernel,
            grid=(count,),
            in_specs=[
                pl.BlockSpec((CHUNK, channels), lambda i: (first + i, 0)),
                pl.BlockSpec((CHUNK, 2 * LANES), lambda i: (first + i, 0)),
                pl.BlockSpec((CHUNK, channels), lambda i: (first + i, 0)),
                pl.BlockSpec((1, 2 * heads, CHUNK), lambda i: (first + i, 0, 0)),
                pl.BlockSpec((1, 6 * heads, CHUNK), lambda i: (first + i, 0, 0)),
                whole((2 * heads, channels)),
                whole((LANES, channels)),
                any_spec,
            ]
            + [any_spec] * len(held),
            out_specs=(
                pl.BlockSpec((CHUNK, channels), lambda i: (first + i, 0)),
                pl.BlockSpec((CHUNK, channels), lambda i: (first + i, 0)),
                whole((LANES, channels)),
            ),
            out_shape=(
                jax.ShapeDtypeStruct((tokens, channels), BF16),
                jax.ShapeDtypeStruct((tokens, channels), BF16),
                jax.ShapeDtypeStruct((LANES, channels), F32),
            ),
            input_output_aliases={8 + k: k for k in range(len(held))},
            scratch_shapes=[pltpu.VMEM((LANES, channels), BF16)],
            compiler_params=params(24),
            cost_estimate=cost(count * 3 * 10**8, count * 10**6, count * 4 * 10**5),
        )(filtered, coupled, gate_values, rows, ex, spread, state, order, *held)

    half = chunks // 2
    gathered = lax.all_to_all(ends, "seq", 0, 0, tiled=True)
    yg, gp, state = inside(0, half, jnp.zeros((LANES, channels), F32), dsec)
    starts = pl.pallas_call(
        relay_kernel,
        grid=(1,),
        in_specs=[whole((sections, share + 8, channels)), any_spec],
        out_specs=whole((sections, share, channels)),
        out_shape=jax.ShapeDtypeStruct((sections, share, channels), BF16),
        compiler_params=params(8),
        cost_estimate=cost(10**6, 10**6),
    )(gathered, state)
    entering = lax.all_to_all(starts, "seq", 0, 0, tiled=True).reshape(LANES, channels)
    yg, gp, _ = inside(half, chunks - half, state, starts, yg, gp)

    gated, squares = pl.pallas_call(
        gated_kernel,
        grid=(tokens // block,),
        in_specs=[
            pl.BlockSpec((block, LANES), lambda i: (i, 1)),
            whole((LANES, channels)),
            pl.BlockSpec((block, channels), lambda i: (i, 0)),
            pl.BlockSpec((block, channels), lambda i: (i, 0)),
        ],
        out_specs=(
            pl.BlockSpec((block, channels), lambda i: (i, 0)),
            whole((groups, chunks, CHUNK)),
        ),
        out_shape=(
            jax.ShapeDtypeStruct((tokens, channels), BF16),
            jax.ShapeDtypeStruct((groups, chunks, CHUNK), F32),
        ),
        scratch_shapes=[pltpu.VMEM((chunks, CHUNK), F32)],
        compiler_params=params(16),
        cost_estimate=cost(6 * 10**8, 12 * 10**6),
    )(coupled, entering, yg, gp)
    squares = lax.all_to_all(squares, "mp", 0, 0, tiled=True)

    return pl.pallas_call(
        functools.partial(normal_kernel, float(channels * groups)),
        grid=(tokens // block,),
        in_specs=[
            pl.BlockSpec((block, channels), lambda i: (i, 0)),
            whole((groups, chunks, CHUNK)),
            whole((1, channels)),
        ],
        out_specs=pl.BlockSpec((block, channels), lambda i: (i, 0)),
        out_shape=jax.ShapeDtypeStruct((tokens, channels), BF16),
        scratch_shapes=[pltpu.VMEM((chunks, CHUNK, LANES), F32)],
        compiler_params=params(16),
        cost_estimate=cost(10**7, 8 * 10**6),
    )(gated, squares, norm_gain[None, :])


def solution(mesh):
    in_specs = (
        P("seq", "mp"),
        P("seq", None),
        P("seq", "mp"),
        P("mp", "seq"),
        P("mp"),
        P(None, "mp"),
        P("mp"),
        P(),
        P(),
        P("mp"),
    )
    out_specs = P("seq", "mp")
    return jax.shard_map(
        on_device, mesh=mesh, in_specs=in_specs, out_specs=out_specs, check_vma=False
    )
```

```python
import functools
import math

import jax
import jax.numpy as jnp
import numpy as np
from jax import lax
from jax.experimental import pallas as pl
from jax.experimental.pallas import tpu as pltpu
from jax.sharding import PartitionSpec as P

CHUNK = 128
LANES = 128
HALO = 8
HEAD_DIM = 64
LOG2E = math.log2(math.e)
BF16 = jnp.bfloat16
F32 = jnp.float32


def params(mib, **flags):
    return pltpu.CompilerParams(vmem_limit_bytes=mib << 20, flags=flags or None)


def far(x):
    return pltpu.with_memory_space_constraint(x, pltpu.HBM)


def cost(flops, nbytes, trans=0):
    return pl.CostEstimate(flops=flops, bytes_accessed=nbytes, transcendentals=trans)


def split(v):
    high = v.astype(BF16)
    return high, (v - high.astype(F32)).astype(BF16)


def contract_rows(a, b):
    return lax.dot_general(a, b, (((0,), (0,)), ((), ())), preferred_element_type=F32)


def contract_lanes(a, b):
    return lax.dot_general(a, b, (((1,), (1,)), ((), ())), preferred_element_type=F32)


def tail_kernel(feat_ref, coup_ref, out_ref):
    channels = feat_ref.shape[1]
    out_ref[:, :channels] = feat_ref[...]
    out_ref[:, channels:] = coup_ref[...]


def decay_kernel(raw_ref, mag_ref, row_ref, wch_ref, ex_ref, run_ref, table_ref):
    heads, tokens = raw_ref.shape
    chunks = tokens // CHUNK
    raw = raw_ref[...]
    small = jnp.exp(-jnp.abs(raw))
    grown = 1.0 + small
    rest = grown - 1.0
    safe = jnp.where(rest == 0.0, 1.0, rest)
    log1p = jnp.where(rest == 0.0, small, jnp.log(grown) * (small / safe))
    step = jnp.maximum(raw, 0.0) + log1p
    diagonal = lax.broadcasted_iota(jnp.int32, (heads, heads), 0) == lax.broadcasted_iota(
        jnp.int32, (heads, heads), 1
    )
    slope = -LOG2E * jnp.sum(jnp.where(diagonal, jnp.exp(mag_ref[...]), 0.0), axis=1, keepdims=True)
    stacked = jnp.concatenate(
        [step[:, c * CHUNK : (c + 1) * CHUNK] for c in range(chunks)], axis=0
    )
    slopes = jnp.concatenate([slope] * chunks, axis=0)
    source = lax.broadcasted_iota(jnp.int32, (CHUNK, 2 * CHUNK), 0)
    target = lax.broadcasted_iota(jnp.int32, (CHUNK, 2 * CHUNK), 1)
    tri = ((target < CHUNK) & (source <= target)) | ((target >= CHUNK) & (source > target - CHUNK))
    sums = jnp.dot(
        stacked * slopes,
        jnp.where(tri, 1.0, 0.0),
        precision=lax.Precision.HIGHEST,
        preferred_element_type=F32,
    )
    lane = lax.broadcasted_iota(jnp.int32, (heads, LANES), 1)
    before = jnp.zeros((heads, 1), F32)
    decays = jnp.zeros((heads, LANES), F32)
    for c in range(chunks):
        rows = slice(c * heads, (c + 1) * heads)
        total = sums[rows, CHUNK - 1 : CHUNK]
        decays = jnp.where(lane == c, total, decays)
        upto = sums[rows, :CHUNK]
        amount = stacked[rows]
        row_ref[c, 0:heads] = upto
        row_ref[c, heads : 2 * heads] = amount
        high, low = split(amount * jnp.exp2(sums[rows, CHUNK:]))
        wch_ref[c, 0:heads] = high
        wch_ref[c, heads : 2 * heads] = low
        high, low = split(jnp.exp2(upto))
        ex_ref[c, 0:heads] = high
        ex_ref[c, heads : 2 * heads] = low
        high, low = split(jnp.exp2(upto + before))
        run_ref[c, 0:heads] = high
        run_ref[c, heads : 2 * heads] = low
        before = before + total
    high, low = split(jnp.exp2(jnp.where(lane == chunks, before, decays)))
    table_ref[0:heads] = high
    table_ref[heads : 2 * heads] = low


def mixed(ext_ref, tile, first, taps, bias):
    start = first + HALO - 3
    half = jnp.broadcast_to(0.5 * bias, (CHUNK, LANES))
    halves = 0.5 * taps
    for k in range(4):
        half = half + halves[k : k + 1] * ext_ref[tile, start + k : start + k + CHUNK, :]
    return half + half * jnp.tanh(half)


def ends_kernel(
    feat_ref, coup_ref, halo_ref, taps_ref, bias_ref, ctaps_ref, cbias_ref, wch_ref, table_ref, spread_ref,
    filt_ref, coupled_ref, states_ref, pay_ref, ext_ref, acc_ref, decay_ref,
):
    i = pl.program_id(0)
    length, channels = feat_ref.shape
    tiles = channels // LANES
    ctiles = coup_ref.shape[1] // LANES
    per = length // CHUNK
    width = 2 * LANES

    @pl.when(i == 0)
    def _():
        for j in range(tiles + ctiles):
            ext_ref[j, 0:HALO, :] = halo_ref[:, j * LANES : (j + 1) * LANES].astype(F32)
        acc_ref[...] = jnp.zeros_like(acc_ref)
        decay_ref[...] = contract_rows(table_ref[...], spread_ref[...])

    @pl.when(i > 0)
    def _():
        for j in range(tiles + ctiles):
            ext_ref[j, 0:HALO, :] = ext_ref[j, length : length + HALO, :]

    for j in range(ctiles):
        part = slice(j * LANES, (j + 1) * LANES)
        ext_ref[tiles + j, HALO : HALO + length, :] = coup_ref[:, part].astype(F32)
    for j in range(tiles):
        part = slice(j * LANES, (j + 1) * LANES)
        ext_ref[j, HALO : HALO + length, :] = feat_ref[:, part].astype(F32)
    for c in range(per):
        rows = slice(c * CHUNK, (c + 1) * CHUNK)
        for j in range(ctiles):
            part = slice(j * LANES, (j + 1) * LANES)
            coupled_ref[rows, part] = mixed(
                ext_ref, tiles + j, c * CHUNK, ctaps_ref[:, part], cbias_ref[:, part]
            ).astype(BF16)
        inputs = coupled_ref[rows, :LANES].T
        columns = wch_ref[c].T
        for q in range(channels // width):
            lanes = slice(q * width, (q + 1) * width)
            scale = jnp.dot(columns, spread_ref[:, lanes], preferred_element_type=F32)
            weighted = []
            for p in range(2):
                j = 2 * q + p
                part = slice(j * LANES, (j + 1) * LANES)
                value = mixed(ext_ref, j, c * CHUNK, taps_ref[:, part], bias_ref[:, part])
                filt_ref[rows, part] = value.astype(BF16)
                weighted.append((value * scale[:, p * LANES : (p + 1) * LANES]).astype(BF16))
            state = acc_ref[:, lanes]
            states_ref[c, :, lanes] = state.astype(BF16)
            decay = decay_ref[pl.ds(i * per + c, 1), lanes]
            acc_ref[:, lanes] = state * decay + jnp.dot(
                inputs, jnp.concatenate(weighted, axis=1), preferred_element_type=F32
            )

    @pl.when(i == pl.num_programs(0) - 1)
    def _():
        final = per * pl.num_programs(0)
        high, low = split(decay_ref[final : final + 1])
        rank = lax.broadcasted_iota(jnp.int32, (8, channels), 0)
        decays = jnp.where(rank == 6, high.astype(F32), low.astype(F32))
        parts = pay_ref.shape[0]
        share = LANES // parts
        for j in range(parts):
            pay_ref[j, 0:share] = acc_ref[j * share : (j + 1) * share].astype(BF16)
            rest = split(acc_ref[j * share : j * share + 8])[1].astype(F32)
            pay_ref[j, share : share + 8] = jnp.where(rank < 6, rest, decays).astype(BF16)


def relay_kernel(pay_ref, order_ref, out_ref):
    parts, rows, channels = pay_ref.shape
    share = rows - 8
    rank = lax.broadcasted_iota(jnp.int32, (8, channels), 0)
    entering = jnp.zeros(out_ref.shape[1:], F32)
    for j in range(parts):
        out_ref[j] = entering
        tail = pay_ref[j, share : share + 8].astype(F32)
        decay = tail[6:7] + tail[7:8]
        ends = pay_ref[j, 0:8].astype(F32) + jnp.where(rank < 6, tail, 0.0)
        if share > 8:
            ends = jnp.concatenate([ends, pay_ref[j, 8:share].astype(F32)], axis=0)
        entering = decay * entering + ends


def inside_kernel(filt_ref, coupled_ref, row_ref, ex_ref, states_ref, spread_ref, order_ref, *rest):
    out_ref = rest[-1]
    heads = row_ref.shape[1] // 2
    length, channels = filt_ref.shape
    above = lax.broadcasted_iota(jnp.int32, (CHUNK, CHUNK), 0)
    below = lax.broadcasted_iota(jnp.int32, (CHUNK, CHUNK), 1)
    lane = lax.broadcasted_iota(jnp.int32, (CHUNK, LANES), 1)
    left = lane < HEAD_DIM
    width = 2 * LANES
    chunks = []
    for c in range(length // CHUNK):
        rows = slice(c * CHUNK, (c + 1) * CHUNK)
        reads = coupled_ref[rows, LANES:]
        scores = jnp.where(above >= below, contract_lanes(reads, coupled_ref[rows, :LANES]), 0.0)
        chunks.append((c, rows, reads, scores, row_ref[c, 0:heads].T, ex_ref[c].T))

    def part(q, c, rows, reads, scores, columns, decays):
        lanes = slice(q * width, (q + 1) * width)
        decayed = jnp.dot(decays, spread_ref[:, lanes], preferred_element_type=F32)
        carried = jnp.dot(reads, states_ref[c, :, lanes], preferred_element_type=F32) * decayed
        for p in range(2):
            weights = []
            for h in (4 * q + 2 * p, 4 * q + 2 * p + 1):
                gap = jnp.minimum(columns[:, h : h + 1] - row_ref[c, h : h + 1], 0.0)
                amount = row_ref[c, heads + h : heads + h + 1]
                weights.append((jnp.exp2(gap) * scores * amount).astype(BF16))
            start = q * width + p * LANES
            pair = filt_ref[rows, start : start + LANES]
            inside = jnp.dot(jnp.concatenate(weights, axis=0), pair, preferred_element_type=F32)
            inside = jnp.where(left, inside[:CHUNK], inside[CHUNK:])
            out_ref[rows, start : start + LANES] = (
                carried[:, p * LANES : (p + 1) * LANES] + inside
            ).astype(BF16)

    for q in range(channels // width):
        for held in chunks:
            part(q, *held)


def gated_kernel(
    read_ref, enter_ref, value_ref, gate_ref, run_ref, spread_ref, gain_ref, gated_ref, out_ref, sums_ref,
    parts_ref,
):
    i = pl.program_id(0)

    @pl.when(i == 0)
    def _():
        high, low = split(enter_ref[...])
        parts_ref[0:LANES] = high
        parts_ref[LANES : 2 * LANES] = low

    length, channels = value_ref.shape
    per = length // CHUNK
    columns = jnp.concatenate([run_ref[c].T for c in range(per)], axis=0)
    reads = jnp.concatenate([read_ref[...], read_ref[...]], axis=1)
    rows = slice(0, length)
    squares = jnp.zeros((length, LANES), F32)
    width = 2 * LANES
    for q in range(channels // width):
        lanes = slice(q * width, (q + 1) * width)
        running = jnp.dot(columns, spread_ref[:, lanes], preferred_element_type=F32)
        before = jnp.dot(reads, parts_ref[:, lanes], preferred_element_type=F32)
        half = (gate_ref[rows, lanes] * 0.5).astype(F32)
        opened = half + half * jnp.tanh(half)
        gated = (value_ref[rows, lanes].astype(F32) + running * before) * opened
        gated_ref[rows, lanes] = (gated * gain_ref[:, lanes]).astype(BF16)
        squares = squares + gated[:, :LANES] * gated[:, :LANES]
        squares = squares + gated[:, LANES:] * gated[:, LANES:]
    totals = contract_lanes(jnp.ones((8, LANES), BF16), squares.astype(BF16))
    for c in range(per):
        sums_ref[pl.ds(i * per + c, 1), :] = totals[0:1, c * CHUNK : (c + 1) * CHUNK]

    @pl.when(i == pl.num_programs(0) - 1)
    def _():
        mine = sums_ref[...].astype(out_ref.dtype)
        for j in range(out_ref.shape[0]):
            out_ref[j] = mine


def normal_kernel(inner, gated_ref, sums_ref, out_ref, scale_ref):
    i = pl.program_id(0)
    length, channels = gated_ref.shape
    chunks = sums_ref.shape[1]

    @pl.when(i == 0)
    def _():
        total = sums_ref[0].astype(F32)
        for j in range(1, sums_ref.shape[0]):
            total = total + sums_ref[j].astype(F32)
        columns = lax.rsqrt(total / inner + 1e-05).T
        for c in range(chunks):
            scale_ref[c] = jnp.broadcast_to(columns[:, c : c + 1], (CHUNK, LANES))

    per = length // CHUNK
    for c in range(per):
        rows = slice(c * CHUNK, (c + 1) * CHUNK)
        scale = scale_ref[i * per + c]
        for j in range(channels // LANES):
            lanes = slice(j * LANES, (j + 1) * LANES)
            out_ref[rows, lanes] = (gated_ref[rows, lanes].astype(F32) * scale).astype(BF16)


def whole(shape):
    return pl.BlockSpec(shape, lambda i: (0,) * len(shape))


def on_device(
    features,
    coupling,
    gate_values,
    step_raw,
    decay_log,
    feature_taps,
    feature_offset,
    coupling_taps,
    coupling_offset,
    norm_gain,
):
    tokens, channels = features.shape
    heads = decay_log.shape[0]
    sections = lax.axis_size("seq")
    groups = lax.axis_size("mp")
    chunks = tokens // CHUNK
    share = LANES // sections
    any_spec = pl.BlockSpec(memory_space=pl.ANY)

    block = 2 * CHUNK
    tail = pl.pallas_call(
        tail_kernel,
        grid=(1,),
        in_specs=[
            pl.BlockSpec((HALO, channels), lambda i: (tokens // HALO - 1, 0)),
            pl.BlockSpec((HALO, 2 * LANES), lambda i: (tokens // HALO - 1, 0)),
        ],
        out_specs=whole((HALO, channels + 2 * LANES)),
        out_shape=pltpu.VMEM((HALO, channels + 2 * LANES), BF16),
        compiler_params=params(4),
        cost_estimate=cost(10**4, 5 * 10**4),
    )(far(features), far(coupling))
    halo = lax.ppermute(tail, "seq", [(i, i + 1) for i in range(sections - 1)])

    one = np.arange(channels)[None, :] // HEAD_DIM == np.arange(heads)[:, None]
    spread = jnp.asarray(np.concatenate([one, one], axis=0), BF16)

    rows, wch, ex, run, table = pl.pallas_call(
        decay_kernel,
        grid=(1,),
        in_specs=[whole((heads, tokens)), whole((1, heads))],
        out_specs=(
            whole((chunks, 2 * heads, CHUNK)),
            whole((chunks, 2 * heads, CHUNK)),
            whole((chunks, 2 * heads, CHUNK)),
            whole((chunks, 2 * heads, CHUNK)),
            whole((2 * heads, LANES)),
        ),
        out_shape=(
            pltpu.VMEM((chunks, 2 * heads, CHUNK), F32),
            pltpu.VMEM((chunks, 2 * heads, CHUNK), BF16),
            pltpu.VMEM((chunks, 2 * heads, CHUNK), BF16),
            pltpu.VMEM((chunks, 2 * heads, CHUNK), BF16),
            pltpu.VMEM((2 * heads, LANES), BF16),
        ),
        compiler_params=params(8),
        cost_estimate=cost(10**7, 10**6, 10**5),
    )(far(step_raw), decay_log[None, :])

    filtered, coupled, states, ends = pl.pallas_call(
        ends_kernel,
        grid=(tokens // block,),
        in_specs=[
            pl.BlockSpec((block, channels), lambda i: (i, 0)),
            pl.BlockSpec((block, 2 * LANES), lambda i: (i, 0)),
            whole((HALO, channels + 2 * LANES)),
            whole((4, channels)),
            whole((1, channels)),
            whole((4, 2 * LANES)),
            whole((1, 2 * LANES)),
            pl.BlockSpec((2, 2 * heads, CHUNK), lambda i: (i, 0, 0)),
            whole((2 * heads, LANES)),
            whole((2 * heads, channels)),
        ],
        out_specs=(
            pl.BlockSpec((block, channels), lambda i: (i, 0)),
            pl.BlockSpec((block, 2 * LANES), lambda i: (i, 0)),
            pl.BlockSpec((2, LANES, channels), lambda i: (i, 0, 0)),
            whole((sections, share + 8, channels)),
        ),
        out_shape=(
            pltpu.HBM((tokens, channels), BF16),
            pltpu.HBM((tokens, 2 * LANES), BF16),
            pltpu.HBM((chunks, LANES, channels), BF16),
            jax.ShapeDtypeStruct((sections, share + 8, channels), BF16),
        ),
        scratch_shapes=[
            pltpu.VMEM((channels // LANES + 2, HALO + block, LANES), F32),
            pltpu.VMEM((LANES, channels), F32),
            pltpu.VMEM((LANES, channels), F32),
        ],
        compiler_params=params(24),
        cost_estimate=cost(10**9, 10**7, 2 * 10**6),
    )(
        far(features),
        far(coupling),
        halo,
        far(feature_taps),
        far(feature_offset[None, :]),
        far(coupling_taps),
        far(coupling_offset[None, :]),
        wch,
        table,
        far(spread),
    )

    def inside(first, count, order, *held):
        return pl.pallas_call(
            inside_kernel,
            grid=(count,),
            in_specs=[
                pl.BlockSpec((block, channels), lambda i: (first + i, 0)),
                pl.BlockSpec((block, 2 * LANES), lambda i: (first + i, 0)),
                pl.BlockSpec((2, 2 * heads, CHUNK), lambda i: (first + i, 0, 0)),
                pl.BlockSpec((2, 2 * heads, CHUNK), lambda i: (first + i, 0, 0)),
                pl.BlockSpec((2, LANES, channels), lambda i: (first + i, 0, 0)),
                whole((2 * heads, channels)),
                any_spec,
            ]
            + [any_spec] * len(held),
            out_specs=pl.BlockSpec((block, channels), lambda i: (first + i, 0)),
            out_shape=pltpu.HBM((tokens, channels), BF16),
            input_output_aliases={7 + k: k for k in range(len(held))},
            compiler_params=params(24),
            cost_estimate=cost(count * 6 * 10**8, count * 2 * 10**6, count * 6 * 10**5),
        )(far(filtered), far(coupled), rows, ex, far(states), far(spread), order, *held)

    steps = tokens // block
    half = steps // 2
    gathered = lax.all_to_all(ends, "seq", 0, 0, tiled=True)
    value = inside(0, half, table)
    starts = pl.pallas_call(
        relay_kernel,
        grid=(1,),
        in_specs=[whole((sections, share + 8, channels)), any_spec],
        out_specs=whole((sections, share, channels)),
        out_shape=jax.ShapeDtypeStruct((sections, share, channels), F32),
        compiler_params=params(8),
        cost_estimate=cost(10**6, 10**6),
    )(gathered, far(value))
    entering = lax.all_to_all(starts, "seq", 0, 0, tiled=True).reshape(LANES, channels)
    value = inside(half, steps - half, starts, far(value))
    gated, squares = pl.pallas_call(
        gated_kernel,
        grid=(tokens // block,),
        in_specs=[
            pl.BlockSpec((block, LANES), lambda i: (i, 1)),
            whole((LANES, channels)),
            pl.BlockSpec((block, channels), lambda i: (i, 0)),
            pl.BlockSpec((block, channels), lambda i: (i, 0)),
            pl.BlockSpec((2, 2 * heads, CHUNK), lambda i: (i, 0, 0)),
            whole((2 * heads, channels)),
            whole((1, channels)),
        ],
        out_specs=(
            pl.BlockSpec((block, channels), lambda i: (i, 0)),
            whole((groups, chunks, CHUNK)),
        ),
        out_shape=(
            pltpu.VMEM((tokens, channels), BF16),
            jax.ShapeDtypeStruct((groups, chunks, CHUNK), BF16),
        ),
        scratch_shapes=[
            pltpu.VMEM((chunks, CHUNK), F32),
            pltpu.VMEM((2 * LANES, channels), BF16),
        ],
        compiler_params=params(16),
        cost_estimate=cost(6 * 10**8, 12 * 10**6),
    )(
        far(coupled), entering, far(value), far(gate_values), run, far(spread), far(norm_gain[None, :])
    )
    squares = lax.all_to_all(squares, "mp", 0, 0, tiled=True)

    return pl.pallas_call(
        functools.partial(normal_kernel, float(channels * groups)),
        grid=(tokens // block,),
        in_specs=[
            pl.BlockSpec((block, channels), lambda i: (i, 0)),
            whole((groups, chunks, CHUNK)),
        ],
        out_specs=pl.BlockSpec((block, channels), lambda i: (i, 0)),
        out_shape=jax.ShapeDtypeStruct((tokens, channels), BF16),
        scratch_shapes=[pltpu.VMEM((chunks, CHUNK, LANES), F32)],
        compiler_params=params(16),
        cost_estimate=cost(10**7, 8 * 10**6),
    )(gated, squares)


def solution(mesh):
    in_specs = (
        P("seq", "mp"),
        P("seq", None),
        P("seq", "mp"),
        P("mp", "seq"),
        P("mp"),
        P(None, "mp"),
        P("mp"),
        P(),
        P(),
        P("mp"),
    )
    out_specs = P("seq", "mp")
    return jax.shard_map(
        on_device, mesh=mesh, in_specs=in_specs, out_specs=out_specs, check_vma=False
    )
```

```python
import functools
import math

import jax
import jax.numpy as jnp
import numpy as np
from jax import lax
from jax.experimental import pallas as pl
from jax.experimental.pallas import tpu as pltpu
from jax.sharding import PartitionSpec as P

CHUNK = 128
LANES = 128
HALO = 8
HEAD_DIM = 64
LOG2E = math.log2(math.e)
BF16 = jnp.bfloat16
F32 = jnp.float32


def params(mib, **flags):
    return pltpu.CompilerParams(vmem_limit_bytes=mib << 20, flags=flags or None)


def far(x):
    return pltpu.with_memory_space_constraint(x, pltpu.HBM)


def cost(flops, nbytes, trans=0):
    return pl.CostEstimate(flops=flops, bytes_accessed=nbytes, transcendentals=trans)


def split(v):
    high = v.astype(BF16)
    return high, (v - high.astype(F32)).astype(BF16)


def contract_rows(a, b):
    return lax.dot_general(a, b, (((0,), (0,)), ((), ())), preferred_element_type=F32)


def contract_lanes(a, b):
    return lax.dot_general(a, b, (((1,), (1,)), ((), ())), preferred_element_type=F32)


def tail_kernel(feat_ref, coup_ref, out_ref):
    channels = feat_ref.shape[1]
    out_ref[:, :channels] = feat_ref[...]
    out_ref[:, channels:] = coup_ref[...]


def decay_kernel(raw_ref, mag_ref, row_ref, wch_ref, ex_ref, run_ref, table_ref):
    heads, tokens = raw_ref.shape
    chunks = tokens // CHUNK
    raw = raw_ref[...]
    small = jnp.exp(-jnp.abs(raw))
    grown = 1.0 + small
    rest = grown - 1.0
    safe = jnp.where(rest == 0.0, 1.0, rest)
    log1p = jnp.where(rest == 0.0, small, jnp.log(grown) * (small / safe))
    step = jnp.maximum(raw, 0.0) + log1p
    diagonal = lax.broadcasted_iota(jnp.int32, (heads, heads), 0) == lax.broadcasted_iota(
        jnp.int32, (heads, heads), 1
    )
    slope = -LOG2E * jnp.sum(jnp.where(diagonal, jnp.exp(mag_ref[...]), 0.0), axis=1, keepdims=True)
    stacked = jnp.concatenate(
        [step[:, c * CHUNK : (c + 1) * CHUNK] for c in range(chunks)], axis=0
    )
    slopes = jnp.concatenate([slope] * chunks, axis=0)
    source = lax.broadcasted_iota(jnp.int32, (CHUNK, 2 * CHUNK), 0)
    target = lax.broadcasted_iota(jnp.int32, (CHUNK, 2 * CHUNK), 1)
    tri = ((target < CHUNK) & (source <= target)) | ((target >= CHUNK) & (source > target - CHUNK))
    sums = jnp.dot(
        stacked * slopes,
        jnp.where(tri, 1.0, 0.0),
        precision=lax.Precision.HIGHEST,
        preferred_element_type=F32,
    )
    lane = lax.broadcasted_iota(jnp.int32, (heads, LANES), 1)
    before = jnp.zeros((heads, 1), F32)
    decays = jnp.zeros((heads, LANES), F32)
    for c in range(chunks):
        rows = slice(c * heads, (c + 1) * heads)
        total = sums[rows, CHUNK - 1 : CHUNK]
        decays = jnp.where(lane == c, total, decays)
        upto = sums[rows, :CHUNK]
        amount = stacked[rows]
        row_ref[c, 0:heads] = upto
        row_ref[c, heads : 2 * heads] = amount
        high, low = split(amount * jnp.exp2(sums[rows, CHUNK:]))
        wch_ref[c, 0:heads] = high
        wch_ref[c, heads : 2 * heads] = low
        high, low = split(jnp.exp2(upto))
        ex_ref[c, 0:heads] = high
        ex_ref[c, heads : 2 * heads] = low
        high, low = split(jnp.exp2(upto + before))
        run_ref[c, 0:heads] = high
        run_ref[c, heads : 2 * heads] = low
        before = before + total
    high, low = split(jnp.exp2(jnp.where(lane == chunks, before, decays)))
    table_ref[0:heads] = high
    table_ref[heads : 2 * heads] = low


def mixed(ext_ref, tile, first, taps, bias):
    start = first + HALO - 3
    half = jnp.broadcast_to(0.5 * bias, (CHUNK, LANES))
    halves = 0.5 * taps
    for k in range(4):
        half = half + halves[k : k + 1] * ext_ref[tile, start + k : start + k + CHUNK, :]
    return half + half * jnp.tanh(half)


def ends_kernel(
    feat_ref, coup_ref, halo_ref, taps_ref, bias_ref, ctaps_ref, cbias_ref, wch_ref, table_ref, spread_ref,
    filt_ref, coupled_ref, states_ref, pay_ref, ext_ref, acc_ref, decay_ref,
):
    i = pl.program_id(0)
    length, channels = feat_ref.shape
    tiles = channels // LANES
    ctiles = coup_ref.shape[1] // LANES
    per = length // CHUNK
    width = 2 * LANES

    @pl.when(i == 0)
    def _():
        for j in range(tiles + ctiles):
            ext_ref[j, 0:HALO, :] = halo_ref[:, j * LANES : (j + 1) * LANES].astype(F32)
        acc_ref[...] = jnp.zeros_like(acc_ref)
        decay_ref[...] = contract_rows(table_ref[...], spread_ref[...])

    @pl.when(i > 0)
    def _():
        for j in range(tiles + ctiles):
            ext_ref[j, 0:HALO, :] = ext_ref[j, length : length + HALO, :]

    for j in range(ctiles):
        part = slice(j * LANES, (j + 1) * LANES)
        ext_ref[tiles + j, HALO : HALO + length, :] = coup_ref[:, part].astype(F32)
    for j in range(tiles):
        part = slice(j * LANES, (j + 1) * LANES)
        ext_ref[j, HALO : HALO + length, :] = feat_ref[:, part].astype(F32)
    for c in range(per):
        rows = slice(c * CHUNK, (c + 1) * CHUNK)
        for j in range(ctiles):
            part = slice(j * LANES, (j + 1) * LANES)
            coupled_ref[rows, part] = mixed(
                ext_ref, tiles + j, c * CHUNK, ctaps_ref[:, part], cbias_ref[:, part]
            ).astype(BF16)
        inputs = coupled_ref[rows, :LANES].T
        columns = wch_ref[c].T
        for q in range(channels // width):
            lanes = slice(q * width, (q + 1) * width)
            scale = jnp.dot(columns, spread_ref[:, lanes], preferred_element_type=F32)
            weighted = []
            for p in range(2):
                j = 2 * q + p
                part = slice(j * LANES, (j + 1) * LANES)
                value = mixed(ext_ref, j, c * CHUNK, taps_ref[:, part], bias_ref[:, part])
                filt_ref[rows, part] = value.astype(BF16)
                weighted.append((value * scale[:, p * LANES : (p + 1) * LANES]).astype(BF16))
            state = acc_ref[:, lanes]
            states_ref[c, :, lanes] = state.astype(BF16)
            decay = decay_ref[pl.ds(i * per + c, 1), lanes]
            acc_ref[:, lanes] = state * decay + jnp.dot(
                inputs, jnp.concatenate(weighted, axis=1), preferred_element_type=F32
            )

    @pl.when(i == pl.num_programs(0) - 1)
    def _():
        final = per * pl.num_programs(0)
        high, low = split(decay_ref[final : final + 1])
        rank = lax.broadcasted_iota(jnp.int32, (8, channels), 0)
        decays = jnp.where(rank == 6, high.astype(F32), low.astype(F32))
        parts = pay_ref.shape[0]
        share = LANES // parts
        for j in range(parts):
            pay_ref[j, 0:share] = acc_ref[j * share : (j + 1) * share].astype(BF16)
            rest = split(acc_ref[j * share : j * share + 8])[1].astype(F32)
            pay_ref[j, share : share + 8] = jnp.where(rank < 6, rest, decays).astype(BF16)


def relay_kernel(pay_ref, order_ref, out_ref):
    parts, rows, channels = pay_ref.shape
    share = rows - 8
    rank = lax.broadcasted_iota(jnp.int32, (8, channels), 0)
    entering = jnp.zeros(out_ref.shape[1:], F32)
    for j in range(parts):
        out_ref[j] = entering
        tail = pay_ref[j, share : share + 8].astype(F32)
        decay = tail[6:7] + tail[7:8]
        ends = pay_ref[j, 0:8].astype(F32) + jnp.where(rank < 6, tail, 0.0)
        if share > 8:
            ends = jnp.concatenate([ends, pay_ref[j, 8:share].astype(F32)], axis=0)
        entering = decay * entering + ends


def inside_kernel(filt_ref, coupled_ref, row_ref, ex_ref, states_ref, spread_ref, order_ref, *rest):
    out_ref = rest[-1]
    heads = row_ref.shape[1] // 2
    length, channels = filt_ref.shape
    above = lax.broadcasted_iota(jnp.int32, (CHUNK, CHUNK), 0)
    below = lax.broadcasted_iota(jnp.int32, (CHUNK, CHUNK), 1)
    lane = lax.broadcasted_iota(jnp.int32, (CHUNK, LANES), 1)
    left = lane < HEAD_DIM
    width = 2 * LANES
    chunks = []
    for c in range(length // CHUNK):
        rows = slice(c * CHUNK, (c + 1) * CHUNK)
        reads = coupled_ref[rows, LANES:]
        scores = jnp.where(above >= below, contract_lanes(reads, coupled_ref[rows, :LANES]), 0.0)
        chunks.append((c, rows, reads, scores, row_ref[c, 0:heads].T, ex_ref[c].T))

    def part(q, c, rows, reads, scores, columns, decays):
        lanes = slice(q * width, (q + 1) * width)
        decayed = jnp.dot(decays, spread_ref[:, lanes], preferred_element_type=F32)
        carried = jnp.dot(reads, states_ref[c, :, lanes], preferred_element_type=F32) * decayed
        for p in range(2):
            weights = []
            for h in (4 * q + 2 * p, 4 * q + 2 * p + 1):
                gap = jnp.minimum(columns[:, h : h + 1] - row_ref[c, h : h + 1], 0.0)
                amount = row_ref[c, heads + h : heads + h + 1]
                weights.append((jnp.exp2(gap) * scores * amount).astype(BF16))
            start = q * width + p * LANES
            pair = filt_ref[rows, start : start + LANES]
            inside = jnp.dot(jnp.concatenate(weights, axis=0), pair, preferred_element_type=F32)
            inside = jnp.where(left, inside[:CHUNK], inside[CHUNK:])
            out_ref[rows, start : start + LANES] = (
                carried[:, p * LANES : (p + 1) * LANES] + inside
            ).astype(BF16)

    for q in range(channels // width):
        for held in chunks:
            part(q, *held)


def gated_kernel(
    coupled_ref, value_ref, gate_ref, enter_ref, run_ref, spread_ref, gated_ref, out_ref,
    read_buf, value_buf, gate_buf, sums_ref, parts_ref, read_sem, value_sem, gate_sem,
):
    steps, length, channels = value_buf.shape
    per = length // CHUNK
    width = 2 * LANES
    reading = pltpu.make_async_copy(coupled_ref.at[:, LANES : 2 * LANES], read_buf, read_sem)

    def arriving(k):
        rows = pl.ds(pl.multiple_of(k * length, length), length)
        return (
            pltpu.make_async_copy(value_ref.at[rows], value_buf.at[k], value_sem.at[k]),
            pltpu.make_async_copy(gate_ref.at[rows], gate_buf.at[k], gate_sem.at[k]),
        )

    for k in range(steps):
        for copy in arriving(k):
            copy.start()
        if k == 0:
            reading.start()
    high, low = split(enter_ref[...])
    parts_ref[0:LANES] = high
    parts_ref[LANES : 2 * LANES] = low
    reading.wait()

    def step(i, carry):
        for copy in arriving(i):
            copy.wait()
        rows = pl.ds(pl.multiple_of(i * length, length), length)
        columns = jnp.concatenate([run_ref[i * per + c].T for c in range(per)], axis=0)
        reads = read_buf[rows]
        reads = jnp.concatenate([reads, reads], axis=1)
        squares = jnp.zeros((length, LANES), F32)
        for q in range(channels // width):
            lanes = slice(q * width, (q + 1) * width)
            running = jnp.dot(columns, spread_ref[:, lanes], preferred_element_type=F32)
            before = jnp.dot(reads, parts_ref[:, lanes], preferred_element_type=F32)
            half = (gate_buf[i, :, lanes] * 0.5).astype(F32)
            opened = half + half * jnp.tanh(half)
            gated = (value_buf[i, :, lanes].astype(F32) + running * before) * opened
            gated_ref[rows, lanes] = gated.astype(BF16)
            squares = squares + gated[:, :LANES] * gated[:, :LANES]
            squares = squares + gated[:, LANES:] * gated[:, LANES:]
        totals = contract_lanes(jnp.ones((8, LANES), BF16), squares.astype(BF16))
        for c in range(per):
            sums_ref[pl.ds(i * per + c, 1), :] = totals[0:1, c * CHUNK : (c + 1) * CHUNK]
        return carry

    lax.fori_loop(0, steps, step, 0)
    mine = sums_ref[...].astype(out_ref.dtype)
    for j in range(out_ref.shape[0]):
        out_ref[j] = mine


def normal_kernel(inner, gated_ref, sums_ref, gain_ref, out_ref, scale_ref, out_buf, out_sem):
    slots, length, channels = out_buf.shape
    steps = gated_ref.shape[0] // length
    per = length // CHUNK
    total = sums_ref[0].astype(F32)
    for j in range(1, sums_ref.shape[0]):
        total = total + sums_ref[j].astype(F32)
    scale_ref[...] = lax.rsqrt(total / inner + 1e-05)

    def leaving(k, slot):
        rows = pl.ds(pl.multiple_of(k * length, length), length)
        return pltpu.make_async_copy(out_buf.at[slot], out_ref.at[rows], out_sem.at[slot])

    def step(i, carry):
        slot = lax.rem(i, slots)

        @pl.when(i >= slots)
        def _():
            leaving(i - slots, slot).wait()

        for c in range(per):
            first = pl.multiple_of(i * length + c * CHUNK, CHUNK)
            scale = jnp.broadcast_to(scale_ref[pl.ds(i * per + c, 1), :], (CHUNK, LANES)).T
            for j in range(channels // LANES):
                lanes = slice(j * LANES, (j + 1) * LANES)
                out_buf[slot, c * CHUNK : (c + 1) * CHUNK, lanes] = (
                    gated_ref[pl.ds(first, CHUNK), lanes].astype(F32) * gain_ref[:, lanes] * scale
                ).astype(BF16)
        leaving(i, slot).start()
        return carry

    lax.fori_loop(0, steps, step, 0)
    for k in range(steps - slots, steps):
        leaving(k, k % slots).wait()


def whole(shape):
    return pl.BlockSpec(shape, lambda i: (0,) * len(shape))


def on_device(
    features,
    coupling,
    gate_values,
    step_raw,
    decay_log,
    feature_taps,
    feature_offset,
    coupling_taps,
    coupling_offset,
    norm_gain,
):
    tokens, channels = features.shape
    heads = decay_log.shape[0]
    sections = lax.axis_size("seq")
    groups = lax.axis_size("mp")
    chunks = tokens // CHUNK
    share = LANES // sections
    any_spec = pl.BlockSpec(memory_space=pl.ANY)

    block = 2 * CHUNK
    tail = pl.pallas_call(
        tail_kernel,
        grid=(1,),
        in_specs=[
            pl.BlockSpec((HALO, channels), lambda i: (tokens // HALO - 1, 0)),
            pl.BlockSpec((HALO, 2 * LANES), lambda i: (tokens // HALO - 1, 0)),
        ],
        out_specs=whole((HALO, channels + 2 * LANES)),
        out_shape=pltpu.VMEM((HALO, channels + 2 * LANES), BF16),
        compiler_params=params(4),
        cost_estimate=cost(10**4, 5 * 10**4),
    )(far(features), far(coupling))
    halo = lax.ppermute(tail, "seq", [(i, i + 1) for i in range(sections - 1)])

    one = np.arange(channels)[None, :] // HEAD_DIM == np.arange(heads)[:, None]
    spread = jnp.asarray(np.concatenate([one, one], axis=0), BF16)

    rows, wch, ex, run, table = pl.pallas_call(
        decay_kernel,
        grid=(1,),
        in_specs=[whole((heads, tokens)), whole((1, heads))],
        out_specs=(
            whole((chunks, 2 * heads, CHUNK)),
            whole((chunks, 2 * heads, CHUNK)),
            whole((chunks, 2 * heads, CHUNK)),
            whole((chunks, 2 * heads, CHUNK)),
            whole((2 * heads, LANES)),
        ),
        out_shape=(
            pltpu.VMEM((chunks, 2 * heads, CHUNK), F32),
            pltpu.VMEM((chunks, 2 * heads, CHUNK), BF16),
            pltpu.VMEM((chunks, 2 * heads, CHUNK), BF16),
            pltpu.VMEM((chunks, 2 * heads, CHUNK), BF16),
            pltpu.VMEM((2 * heads, LANES), BF16),
        ),
        compiler_params=params(8),
        cost_estimate=cost(10**7, 10**6, 10**5),
    )(far(step_raw), decay_log[None, :])

    filtered, coupled, states, ends = pl.pallas_call(
        ends_kernel,
        grid=(tokens // block,),
        in_specs=[
            pl.BlockSpec((block, channels), lambda i: (i, 0)),
            pl.BlockSpec((block, 2 * LANES), lambda i: (i, 0)),
            whole((HALO, channels + 2 * LANES)),
            whole((4, channels)),
            whole((1, channels)),
            whole((4, 2 * LANES)),
            whole((1, 2 * LANES)),
            pl.BlockSpec((2, 2 * heads, CHUNK), lambda i: (i, 0, 0)),
            whole((2 * heads, LANES)),
            whole((2 * heads, channels)),
        ],
        out_specs=(
            pl.BlockSpec((block, channels), lambda i: (i, 0)),
            pl.BlockSpec((block, 2 * LANES), lambda i: (i, 0)),
            pl.BlockSpec((2, LANES, channels), lambda i: (i, 0, 0)),
            whole((sections, share + 8, channels)),
        ),
        out_shape=(
            pltpu.HBM((tokens, channels), BF16),
            pltpu.HBM((tokens, 2 * LANES), BF16),
            pltpu.HBM((chunks, LANES, channels), BF16),
            jax.ShapeDtypeStruct((sections, share + 8, channels), BF16),
        ),
        scratch_shapes=[
            pltpu.VMEM((channels // LANES + 2, HALO + block, LANES), F32),
            pltpu.VMEM((LANES, channels), F32),
            pltpu.VMEM((LANES, channels), F32),
        ],
        compiler_params=params(24),
        cost_estimate=cost(10**9, 10**7, 2 * 10**6),
    )(
        far(features),
        far(coupling),
        halo,
        far(feature_taps),
        far(feature_offset[None, :]),
        far(coupling_taps),
        far(coupling_offset[None, :]),
        wch,
        table,
        far(spread),
    )

    def inside(first, count, order, *held):
        return pl.pallas_call(
            inside_kernel,
            grid=(count,),
            in_specs=[
                pl.BlockSpec((block, channels), lambda i: (first + i, 0)),
                pl.BlockSpec((block, 2 * LANES), lambda i: (first + i, 0)),
                pl.BlockSpec((2, 2 * heads, CHUNK), lambda i: (first + i, 0, 0)),
                pl.BlockSpec((2, 2 * heads, CHUNK), lambda i: (first + i, 0, 0)),
                pl.BlockSpec((2, LANES, channels), lambda i: (first + i, 0, 0)),
                whole((2 * heads, channels)),
                any_spec,
            ]
            + [any_spec] * len(held),
            out_specs=pl.BlockSpec((block, channels), lambda i: (first + i, 0)),
            out_shape=pltpu.HBM((tokens, channels), BF16),
            input_output_aliases={7 + k: k for k in range(len(held))},
            compiler_params=params(24),
            cost_estimate=cost(count * 6 * 10**8, count * 2 * 10**6, count * 6 * 10**5),
        )(far(filtered), far(coupled), rows, ex, far(states), far(spread), order, *held)

    steps = tokens // block
    half = steps // 2
    gathered = lax.all_to_all(ends, "seq", 0, 0, tiled=True)
    value = inside(0, half, table)
    starts = pl.pallas_call(
        relay_kernel,
        grid=(1,),
        in_specs=[whole((sections, share + 8, channels)), any_spec],
        out_specs=whole((sections, share, channels)),
        out_shape=jax.ShapeDtypeStruct((sections, share, channels), F32),
        compiler_params=params(8),
        cost_estimate=cost(10**6, 10**6),
    )(gathered, far(value))
    entering = lax.all_to_all(starts, "seq", 0, 0, tiled=True).reshape(LANES, channels)
    value = inside(half, steps - half, starts, far(value))
    near_spec = pl.BlockSpec(memory_space=pltpu.VMEM)
    gated, squares = pl.pallas_call(
        gated_kernel,
        in_specs=[any_spec] * 3 + [near_spec] * 3,
        out_specs=(near_spec, near_spec),
        out_shape=(
            pltpu.VMEM((tokens, channels), BF16),
            pltpu.VMEM((groups, chunks, CHUNK), BF16),
        ),
        scratch_shapes=[
            pltpu.VMEM((tokens, LANES), BF16),
            pltpu.VMEM((tokens // block, block, channels), BF16),
            pltpu.VMEM((tokens // block, block, channels), BF16),
            pltpu.VMEM((chunks, CHUNK), F32),
            pltpu.VMEM((2 * LANES, channels), BF16),
            pltpu.SemaphoreType.DMA,
            pltpu.SemaphoreType.DMA((tokens // block,)),
            pltpu.SemaphoreType.DMA((tokens // block,)),
        ],
        compiler_params=params(24),
        cost_estimate=cost(6 * 10**8, 12 * 10**6),
    )(far(coupled), far(value), far(gate_values), entering, run, spread)
    squares = lax.all_to_all(squares, "mp", 0, 0, tiled=True)

    slots = min(4, tokens // block)
    return pl.pallas_call(
        functools.partial(normal_kernel, float(channels * groups)),
        in_specs=[near_spec] * 3,
        out_specs=any_spec,
        out_shape=jax.ShapeDtypeStruct((tokens, channels), BF16),
        scratch_shapes=[
            pltpu.VMEM((chunks, CHUNK), F32),
            pltpu.VMEM((slots, block, channels), BF16),
            pltpu.SemaphoreType.DMA((slots,)),
        ],
        compiler_params=params(16),
        cost_estimate=cost(10**7, 8 * 10**6),
    )(gated, squares, norm_gain[None, :])


def solution(mesh):
    in_specs = (
        P("seq", "mp"),
        P("seq", None),
        P("seq", "mp"),
        P("mp", "seq"),
        P("mp"),
        P(None, "mp"),
        P("mp"),
        P(),
        P(),
        P("mp"),
    )
    out_specs = P("seq", "mp")
    return jax.shard_map(
        on_device, mesh=mesh, in_specs=in_specs, out_specs=out_specs, check_vma=False
    )
```

```python
import functools
import math

import jax
import jax.numpy as jnp
import numpy as np
from jax import lax
from jax.experimental import pallas as pl
from jax.experimental.pallas import tpu as pltpu
from jax.sharding import PartitionSpec as P

CHUNK = 128
LANES = 128
HALO = 8
HEAD_DIM = 64
LOG2E = math.log2(math.e)
BF16 = jnp.bfloat16
F32 = jnp.float32


def params(mib, **flags):
    return pltpu.CompilerParams(vmem_limit_bytes=mib << 20, flags=flags or None)


def far(x):
    return pltpu.with_memory_space_constraint(x, pltpu.HBM)


def cost(flops, nbytes, trans=0):
    return pl.CostEstimate(flops=flops, bytes_accessed=nbytes, transcendentals=trans)


def split(v):
    high = v.astype(BF16)
    return high, (v - high.astype(F32)).astype(BF16)


def contract_rows(a, b):
    return lax.dot_general(a, b, (((0,), (0,)), ((), ())), preferred_element_type=F32)


def contract_lanes(a, b):
    return lax.dot_general(a, b, (((1,), (1,)), ((), ())), preferred_element_type=F32)


def tail_kernel(feat_ref, coup_ref, out_ref):
    channels = feat_ref.shape[1]
    out_ref[:, :channels] = feat_ref[...]
    out_ref[:, channels:] = coup_ref[...]


def decay_kernel(raw_ref, mag_ref, row_ref, wch_ref, ex_ref, run_ref, table_ref):
    heads, tokens = raw_ref.shape
    chunks = tokens // CHUNK
    raw = raw_ref[...]
    small = jnp.exp(-jnp.abs(raw))
    grown = 1.0 + small
    rest = grown - 1.0
    safe = jnp.where(rest == 0.0, 1.0, rest)
    log1p = jnp.where(rest == 0.0, small, jnp.log(grown) * (small / safe))
    step = jnp.maximum(raw, 0.0) + log1p
    diagonal = lax.broadcasted_iota(jnp.int32, (heads, heads), 0) == lax.broadcasted_iota(
        jnp.int32, (heads, heads), 1
    )
    slope = -LOG2E * jnp.sum(jnp.where(diagonal, jnp.exp(mag_ref[...]), 0.0), axis=1, keepdims=True)
    stacked = jnp.concatenate(
        [step[:, c * CHUNK : (c + 1) * CHUNK] for c in range(chunks)], axis=0
    )
    slopes = jnp.concatenate([slope] * chunks, axis=0)
    source = lax.broadcasted_iota(jnp.int32, (CHUNK, 2 * CHUNK), 0)
    target = lax.broadcasted_iota(jnp.int32, (CHUNK, 2 * CHUNK), 1)
    tri = ((target < CHUNK) & (source <= target)) | ((target >= CHUNK) & (source > target - CHUNK))
    sums = jnp.dot(
        stacked * slopes,
        jnp.where(tri, 1.0, 0.0),
        precision=lax.Precision.HIGHEST,
        preferred_element_type=F32,
    )
    lane = lax.broadcasted_iota(jnp.int32, (heads, LANES), 1)
    before = jnp.zeros((heads, 1), F32)
    decays = jnp.zeros((heads, LANES), F32)
    for c in range(chunks):
        rows = slice(c * heads, (c + 1) * heads)
        total = sums[rows, CHUNK - 1 : CHUNK]
        decays = jnp.where(lane == c, total, decays)
        upto = sums[rows, :CHUNK]
        amount = stacked[rows]
        row_ref[c, 0:heads] = upto
        row_ref[c, heads : 2 * heads] = amount
        high, low = split(amount * jnp.exp2(sums[rows, CHUNK:]))
        wch_ref[c, 0:heads] = high
        wch_ref[c, heads : 2 * heads] = low
        high, low = split(jnp.exp2(upto))
        ex_ref[c, 0:heads] = high
        ex_ref[c, heads : 2 * heads] = low
        high, low = split(jnp.exp2(upto + before))
        run_ref[c, 0:heads] = high
        run_ref[c, heads : 2 * heads] = low
        before = before + total
    high, low = split(jnp.exp2(jnp.where(lane == chunks, before, decays)))
    table_ref[0:heads] = high
    table_ref[heads : 2 * heads] = low


def mixed(ext_ref, tile, first, taps, bias):
    start = first + HALO - 3
    half = jnp.broadcast_to(0.5 * bias, (CHUNK, LANES))
    halves = 0.5 * taps
    for k in range(4):
        half = half + halves[k : k + 1] * ext_ref[tile, start + k : start + k + CHUNK, :]
    return half + half * jnp.tanh(half)


def ends_kernel(
    feat_ref, coup_ref, halo_ref, taps_ref, bias_ref, ctaps_ref, cbias_ref, wch_ref, table_ref, spread_ref,
    filt_ref, coupled_ref, states_ref, pay_ref, ext_ref, acc_ref, decay_ref,
):
    i = pl.program_id(0)
    length, channels = feat_ref.shape
    tiles = channels // LANES
    ctiles = coup_ref.shape[1] // LANES
    per = length // CHUNK
    width = 2 * LANES

    @pl.when(i == 0)
    def _():
        for j in range(tiles + ctiles):
            ext_ref[j, 0:HALO, :] = halo_ref[:, j * LANES : (j + 1) * LANES].astype(F32)
        acc_ref[...] = jnp.zeros_like(acc_ref)
        decay_ref[...] = contract_rows(table_ref[...], spread_ref[...])

    @pl.when(i > 0)
    def _():
        for j in range(tiles + ctiles):
            ext_ref[j, 0:HALO, :] = ext_ref[j, length : length + HALO, :]

    for j in range(ctiles):
        part = slice(j * LANES, (j + 1) * LANES)
        ext_ref[tiles + j, HALO : HALO + length, :] = coup_ref[:, part].astype(F32)
    for j in range(tiles):
        part = slice(j * LANES, (j + 1) * LANES)
        ext_ref[j, HALO : HALO + length, :] = feat_ref[:, part].astype(F32)
    for c in range(per):
        rows = slice(c * CHUNK, (c + 1) * CHUNK)
        for j in range(ctiles):
            part = slice(j * LANES, (j + 1) * LANES)
            coupled_ref[rows, part] = mixed(
                ext_ref, tiles + j, c * CHUNK, ctaps_ref[:, part], cbias_ref[:, part]
            ).astype(BF16)
        inputs = coupled_ref[rows, :LANES].T
        columns = wch_ref[c].T
        for q in range(channels // width):
            lanes = slice(q * width, (q + 1) * width)
            scale = jnp.dot(columns, spread_ref[:, lanes], preferred_element_type=F32)
            weighted = []
            for p in range(2):
                j = 2 * q + p
                part = slice(j * LANES, (j + 1) * LANES)
                value = mixed(ext_ref, j, c * CHUNK, taps_ref[:, part], bias_ref[:, part])
                filt_ref[rows, part] = value.astype(BF16)
                weighted.append((value * scale[:, p * LANES : (p + 1) * LANES]).astype(BF16))
            state = acc_ref[:, lanes]
            states_ref[c, :, lanes] = state.astype(BF16)
            decay = decay_ref[pl.ds(i * per + c, 1), lanes]
            acc_ref[:, lanes] = state * decay + jnp.dot(
                inputs, jnp.concatenate(weighted, axis=1), preferred_element_type=F32
            )

    @pl.when(i == pl.num_programs(0) - 1)
    def _():
        final = per * pl.num_programs(0)
        high, low = split(decay_ref[final : final + 1])
        rank = lax.broadcasted_iota(jnp.int32, (8, channels), 0)
        decays = jnp.where(rank == 6, high.astype(F32), low.astype(F32))
        parts = pay_ref.shape[0]
        share = LANES // parts
        for j in range(parts):
            pay_ref[j, 0:share] = acc_ref[j * share : (j + 1) * share].astype(BF16)
            rest = split(acc_ref[j * share : j * share + 8])[1].astype(F32)
            pay_ref[j, share : share + 8] = jnp.where(rank < 6, rest, decays).astype(BF16)


def relay_kernel(pay_ref, order_ref, out_ref):
    parts, rows, channels = pay_ref.shape
    share = rows - 8
    rank = lax.broadcasted_iota(jnp.int32, (8, channels), 0)
    entering = jnp.zeros(out_ref.shape[1:], F32)
    for j in range(parts):
        out_ref[j] = entering
        tail = pay_ref[j, share : share + 8].astype(F32)
        decay = tail[6:7] + tail[7:8]
        ends = pay_ref[j, 0:8].astype(F32) + jnp.where(rank < 6, tail, 0.0)
        if share > 8:
            ends = jnp.concatenate([ends, pay_ref[j, 8:share].astype(F32)], axis=0)
        entering = decay * entering + ends


def inside_kernel(filt_ref, coupled_ref, row_ref, ex_ref, states_ref, spread_ref, order_ref, *rest):
    out_ref = rest[-1]
    heads = row_ref.shape[1] // 2
    length, channels = filt_ref.shape
    above = lax.broadcasted_iota(jnp.int32, (CHUNK, CHUNK), 0)
    below = lax.broadcasted_iota(jnp.int32, (CHUNK, CHUNK), 1)
    lane = lax.broadcasted_iota(jnp.int32, (CHUNK, LANES), 1)
    left = lane < HEAD_DIM
    width = 2 * LANES
    chunks = []
    for c in range(length // CHUNK):
        rows = slice(c * CHUNK, (c + 1) * CHUNK)
        reads = coupled_ref[rows, LANES:]
        scores = jnp.where(above >= below, contract_lanes(reads, coupled_ref[rows, :LANES]), 0.0)
        chunks.append((c, rows, reads, scores, row_ref[c, 0:heads].T, ex_ref[c].T))

    def part(q, c, rows, reads, scores, columns, decays):
        lanes = slice(q * width, (q + 1) * width)
        decayed = jnp.dot(decays, spread_ref[:, lanes], preferred_element_type=F32)
        carried = jnp.dot(reads, states_ref[c, :, lanes], preferred_element_type=F32) * decayed
        for p in range(2):
            weights = []
            for h in (4 * q + 2 * p, 4 * q + 2 * p + 1):
                gap = jnp.minimum(columns[:, h : h + 1] - row_ref[c, h : h + 1], 0.0)
                amount = row_ref[c, heads + h : heads + h + 1]
                weights.append((jnp.exp2(gap) * scores * amount).astype(BF16))
            start = q * width + p * LANES
            pair = filt_ref[rows, start : start + LANES]
            inside = jnp.dot(jnp.concatenate(weights, axis=0), pair, preferred_element_type=F32)
            inside = jnp.where(left, inside[:CHUNK], inside[CHUNK:])
            out_ref[rows, start : start + LANES] = (
                carried[:, p * LANES : (p + 1) * LANES] + inside
            ).astype(BF16)

    for q in range(channels // width):
        for held in chunks:
            part(q, *held)


def gated_kernel(
    coupled_ref, value_ref, gate_ref, enter_ref, run_ref, spread_ref, gated_ref, out_ref,
    read_buf, value_buf, gate_buf, sums_ref, parts_ref, read_sem, value_sem, gate_sem,
):
    steps, length, channels = value_buf.shape
    per = length // CHUNK
    width = 2 * LANES
    reading = pltpu.make_async_copy(coupled_ref.at[:, LANES : 2 * LANES], read_buf, read_sem)

    def arriving(k):
        rows = pl.ds(pl.multiple_of(k * length, length), length)
        return (
            pltpu.make_async_copy(value_ref.at[rows], value_buf.at[k], value_sem.at[k]),
            pltpu.make_async_copy(gate_ref.at[rows], gate_buf.at[k], gate_sem.at[k]),
        )

    for k in range(steps):
        for copy in arriving(k):
            copy.start()
        if k == 0:
            reading.start()
    high, low = split(enter_ref[...])
    parts_ref[0:LANES] = high
    parts_ref[LANES : 2 * LANES] = low
    reading.wait()

    def step(i, carry):
        for copy in arriving(i):
            copy.wait()
        rows = pl.ds(pl.multiple_of(i * length, length), length)
        columns = jnp.concatenate([run_ref[i * per + c].T for c in range(per)], axis=0)
        reads = read_buf[rows]
        reads = jnp.concatenate([reads, reads], axis=1)
        squares = jnp.zeros((length, LANES), F32)
        for q in range(channels // width):
            lanes = slice(q * width, (q + 1) * width)
            running = jnp.dot(columns, spread_ref[:, lanes], preferred_element_type=F32)
            before = jnp.dot(reads, parts_ref[:, lanes], preferred_element_type=F32)
            half = (gate_buf[i, :, lanes] * 0.5).astype(F32)
            opened = half + half * jnp.tanh(half)
            gated = (value_buf[i, :, lanes].astype(F32) + running * before) * opened
            gated_ref[rows, lanes] = gated.astype(BF16)
            squares = squares + gated[:, :LANES] * gated[:, :LANES]
            squares = squares + gated[:, LANES:] * gated[:, LANES:]
        totals = contract_lanes(jnp.ones((8, LANES), BF16), squares.astype(BF16))
        for c in range(per):
            sums_ref[pl.ds(i * per + c, 1), :] = totals[0:1, c * CHUNK : (c + 1) * CHUNK]
        return carry

    lax.fori_loop(0, steps, step, 0)
    mine = sums_ref[...].astype(out_ref.dtype)
    for j in range(out_ref.shape[0]):
        out_ref[j] = mine


def normal_kernel(inner, gated_ref, sums_ref, gain_ref, out_ref, scale_ref, out_buf, out_sem):
    slots, length, channels = out_buf.shape
    steps = gated_ref.shape[0] // length
    per = length // CHUNK
    total = sums_ref[0].astype(F32)
    for j in range(1, sums_ref.shape[0]):
        total = total + sums_ref[j].astype(F32)
    scale_ref[...] = lax.rsqrt(total / inner + 1e-05)

    def leaving(k, slot):
        rows = pl.ds(pl.multiple_of(k * length, length), length)
        return pltpu.make_async_copy(out_buf.at[slot], out_ref.at[rows], out_sem.at[slot])

    def step(i, carry):
        slot = lax.rem(i, slots)

        @pl.when(i >= slots)
        def _():
            leaving(i - slots, slot).wait()

        for c in range(per):
            first = pl.multiple_of(i * length + c * CHUNK, CHUNK)
            scale = jnp.broadcast_to(scale_ref[pl.ds(i * per + c, 1), :], (CHUNK, LANES)).T
            for j in range(channels // LANES):
                lanes = slice(j * LANES, (j + 1) * LANES)
                out_buf[slot, c * CHUNK : (c + 1) * CHUNK, lanes] = (
                    gated_ref[pl.ds(first, CHUNK), lanes].astype(F32) * gain_ref[:, lanes] * scale
                ).astype(BF16)
        leaving(i, slot).start()
        return carry

    lax.fori_loop(0, steps, step, 0)
    for k in range(steps - slots, steps):
        leaving(k, k % slots).wait()


def whole(shape):
    return pl.BlockSpec(shape, lambda i: (0,) * len(shape))


def on_device(
    features,
    coupling,
    gate_values,
    step_raw,
    decay_log,
    feature_taps,
    feature_offset,
    coupling_taps,
    coupling_offset,
    norm_gain,
):
    tokens, channels = features.shape
    heads = decay_log.shape[0]
    sections = lax.axis_size("seq")
    groups = lax.axis_size("mp")
    chunks = tokens // CHUNK
    share = LANES // sections
    any_spec = pl.BlockSpec(memory_space=pl.ANY)
    near_spec = pl.BlockSpec(memory_space=pltpu.VMEM)

    block = 2 * CHUNK
    tail = pl.pallas_call(
        tail_kernel,
        grid=(1,),
        in_specs=[
            pl.BlockSpec((HALO, channels), lambda i: (tokens // HALO - 1, 0)),
            pl.BlockSpec((HALO, 2 * LANES), lambda i: (tokens // HALO - 1, 0)),
        ],
        out_specs=whole((HALO, channels + 2 * LANES)),
        out_shape=pltpu.VMEM((HALO, channels + 2 * LANES), BF16),
        compiler_params=params(4),
        cost_estimate=cost(10**4, 5 * 10**4),
    )(far(features), far(coupling))
    halo = lax.ppermute(tail, "seq", [(i, i + 1) for i in range(sections - 1)])

    one = np.arange(channels)[None, :] // HEAD_DIM == np.arange(heads)[:, None]
    spread = jnp.asarray(np.concatenate([one, one], axis=0), BF16)

    rows, wch, ex, run, table = pl.pallas_call(
        decay_kernel,
        in_specs=[near_spec] * 2,
        out_specs=(near_spec,) * 5,
        out_shape=(
            pltpu.VMEM((chunks, 2 * heads, CHUNK), F32),
            pltpu.VMEM((chunks, 2 * heads, CHUNK), BF16),
            pltpu.VMEM((chunks, 2 * heads, CHUNK), BF16),
            pltpu.VMEM((chunks, 2 * heads, CHUNK), BF16),
            pltpu.VMEM((2 * heads, LANES), BF16),
        ),
        compiler_params=params(8),
        cost_estimate=cost(10**7, 10**6, 10**5),
    )(step_raw, decay_log[None, :])

    filtered, coupled, states, ends = pl.pallas_call(
        ends_kernel,
        grid=(tokens // block,),
        in_specs=[
            pl.BlockSpec((block, channels), lambda i: (i, 0)),
            pl.BlockSpec((block, 2 * LANES), lambda i: (i, 0)),
            whole((HALO, channels + 2 * LANES)),
            whole((4, channels)),
            whole((1, channels)),
            whole((4, 2 * LANES)),
            whole((1, 2 * LANES)),
            pl.BlockSpec((2, 2 * heads, CHUNK), lambda i: (i, 0, 0)),
            whole((2 * heads, LANES)),
            whole((2 * heads, channels)),
        ],
        out_specs=(
            pl.BlockSpec((block, channels), lambda i: (i, 0)),
            pl.BlockSpec((block, 2 * LANES), lambda i: (i, 0)),
            pl.BlockSpec((2, LANES, channels), lambda i: (i, 0, 0)),
            whole((sections, share + 8, channels)),
        ),
        out_shape=(
            pltpu.HBM((tokens, channels), BF16),
            pltpu.HBM((tokens, 2 * LANES), BF16),
            pltpu.HBM((chunks, LANES, channels), BF16),
            jax.ShapeDtypeStruct((sections, share + 8, channels), BF16),
        ),
        scratch_shapes=[
            pltpu.VMEM((channels // LANES + 2, HALO + block, LANES), F32),
            pltpu.VMEM((LANES, channels), F32),
            pltpu.VMEM((LANES, channels), F32),
        ],
        compiler_params=params(24),
        cost_estimate=cost(10**9, 10**7, 2 * 10**6),
    )(
        far(features),
        far(coupling),
        halo,
        far(feature_taps),
        far(feature_offset[None, :]),
        far(coupling_taps),
        far(coupling_offset[None, :]),
        wch,
        table,
        far(spread),
    )

    def inside(first, count, order, *held):
        return pl.pallas_call(
            inside_kernel,
            grid=(count,),
            in_specs=[
                pl.BlockSpec((block, channels), lambda i: (first + i, 0)),
                pl.BlockSpec((block, 2 * LANES), lambda i: (first + i, 0)),
                pl.BlockSpec((2, 2 * heads, CHUNK), lambda i: (first + i, 0, 0)),
                pl.BlockSpec((2, 2 * heads, CHUNK), lambda i: (first + i, 0, 0)),
                pl.BlockSpec((2, LANES, channels), lambda i: (first + i, 0, 0)),
                whole((2 * heads, channels)),
                any_spec,
            ]
            + [any_spec] * len(held),
            out_specs=pl.BlockSpec((block, channels), lambda i: (first + i, 0)),
            out_shape=pltpu.HBM((tokens, channels), BF16),
            input_output_aliases={7 + k: k for k in range(len(held))},
            compiler_params=params(24),
            cost_estimate=cost(count * 6 * 10**8, count * 2 * 10**6, count * 6 * 10**5),
        )(far(filtered), far(coupled), rows, ex, far(states), far(spread), order, *held)

    steps = tokens // block
    half = steps // 2
    gathered = lax.all_to_all(ends, "seq", 0, 0, tiled=True)
    value = inside(0, half, table)
    starts = pl.pallas_call(
        relay_kernel,
        in_specs=[near_spec, any_spec],
        out_specs=near_spec,
        out_shape=jax.ShapeDtypeStruct((sections, share, channels), F32),
        compiler_params=params(8),
        cost_estimate=cost(10**6, 10**6),
    )(gathered, far(value))
    entering = lax.all_to_all(starts, "seq", 0, 0, tiled=True).reshape(LANES, channels)
    value = inside(half, steps - half, starts, far(value))
    gated, squares = pl.pallas_call(
        gated_kernel,
        in_specs=[any_spec] * 3 + [near_spec] * 3,
        out_specs=(near_spec, near_spec),
        out_shape=(
            pltpu.VMEM((tokens, channels), BF16),
            pltpu.VMEM((groups, chunks, CHUNK), BF16),
        ),
        scratch_shapes=[
            pltpu.VMEM((tokens, LANES), BF16),
            pltpu.VMEM((tokens // block, block, channels), BF16),
            pltpu.VMEM((tokens // block, block, channels), BF16),
            pltpu.VMEM((chunks, CHUNK), F32),
            pltpu.VMEM((2 * LANES, channels), BF16),
            pltpu.SemaphoreType.DMA,
            pltpu.SemaphoreType.DMA((tokens // block,)),
            pltpu.SemaphoreType.DMA((tokens // block,)),
        ],
        compiler_params=params(24),
        cost_estimate=cost(6 * 10**8, 12 * 10**6),
    )(far(coupled), far(value), far(gate_values), entering, run, spread)
    squares = lax.all_to_all(squares, "mp", 0, 0, tiled=True)

    slots = min(4, tokens // block)
    return pl.pallas_call(
        functools.partial(normal_kernel, float(channels * groups)),
        in_specs=[near_spec] * 3,
        out_specs=any_spec,
        out_shape=jax.ShapeDtypeStruct((tokens, channels), BF16),
        scratch_shapes=[
            pltpu.VMEM((chunks, CHUNK), F32),
            pltpu.VMEM((slots, block, channels), BF16),
            pltpu.SemaphoreType.DMA((slots,)),
        ],
        compiler_params=params(16),
        cost_estimate=cost(10**7, 8 * 10**6),
    )(gated, squares, norm_gain[None, :])


def solution(mesh):
    in_specs = (
        P("seq", "mp"),
        P("seq", None),
        P("seq", "mp"),
        P("mp", "seq"),
        P("mp"),
        P(None, "mp"),
        P("mp"),
        P(),
        P(),
        P("mp"),
    )
    out_specs = P("seq", "mp")
    return jax.shard_map(
        on_device, mesh=mesh, in_specs=in_specs, out_specs=out_specs, check_vma=False
    )
```
